256 devices in a mesh: replica: 2 (over z_lo), segment: 4 (over z_hi), tensor: 32 (over x, y, core).
Axes of the slice: x: 4, y: 4, z: 8 (z_hi: 4, z_lo: 2; z = z_hi * 2 + z_lo), core: 2. Of those that a mesh axis runs over, the one named last changes fastest.
Arguments:
- x_in: bfloat16 [256, 8192], P('replica', 'tensor'), parts along dimension 0, may hold values from -6 to 6
- norm_gain: float32 [4, 8192], P('segment'), may hold values from 0.5 to 1.5
- in_index: int32 [4, 224, 72], P('segment', 'tensor'), may hold values from -1 to 127, as said below
- gate_blocks: bfloat16 [4, 224, 72, 4096], P('segment', 'tensor'), may hold values from -0.09375 to 0.09375
- up_blocks: bfloat16 [4, 224, 72, 4096], P('segment', 'tensor'), may hold values from -0.09375 to 0.09375
- out_index: int32 [4, 128, 126], P('segment', 'tensor'), may hold values from -1 to 223, as said below
- down_blocks: bfloat16 [4, 128, 126, 4096], P('segment', 'tensor'), may hold values from -0.0625 to 0.0625
Outputs:
- sections: bfloat16 [4, 256, 8192], P('segment', 'replica', 'tensor'), parts along dimension 1
The draws below stay inside these ranges and needn't reach their ends.
There are 2 independent parts, one for each index of `replica`. The reference program is written for one: setup_inputs(seed, part) draws one part's arguments, and reference() takes and returns one part's arrays. A program takes and returns all parts, laid end to end along the dimension named above; an argument that names none is the same for every part. Nothing has to cross between parts.
Inputs may be any that keep to these rules, and one draw needn't show every extreme that they name: `in_index`: for each section and column block the entries name distinct row blocks, the kept ones first and -1 in the remaining slots; between 3 * 128 / 8 (rounded down) and 72 slots are kept, and in every section some column block keeps exactly 72 and another exactly the least. `out_index`: for each section and column block the entries name distinct row blocks, the kept ones first and -1 in the remaining slots; between 3 * 224 / 8 (rounded down) and 126 slots are kept, and in every section some column block keeps exactly 126 and another exactly the least.
All inputs are finite; a program needn't handle non-finite values.
Results may differ from the reference program's by a relative error of at most 0.0095.
Values may be sent and summed in bfloat16 or wider, within the bound.
No kernel may reach another device: no remote copies, remote signals or barrier semaphores. Data moves between devices by JAX's collectives and lax.ppermute only.
A program may use at most 128 MiB of HBM per device.

```python
import jax
import jax.numpy as jnp
from jax import lax

D = 8192
FFW = 14336
BS = 64
TOKENS = 128
SEGMENTS = 4
RB_IN = 128
RB_OUT = 224
MAXB = 72
MAXO = 126


def mask_lists(key, tile_count, row_blocks, most_kept):
    least_kept = 3 * row_blocks // 8
    key_perm, key_count, key_highest, key_lowest = jax.random.split(key, 4)
    key_list = jax.random.split(key_perm, SEGMENTS * tile_count)

    def one_order(single_key):
        return jax.random.permutation(single_key, row_blocks)
    orders = jax.vmap(one_order)(key_list)[:, :most_kept]
    orders = orders.reshape(SEGMENTS, tile_count, most_kept).astype(jnp.int32)
    counts = jax.random.randint(key_count, (SEGMENTS, tile_count), least_kept, most_kept + 1)
    highest = jax.random.randint(key_highest, (SEGMENTS, 1), 0, tile_count)
    lowest = (highest + 1 + jax.random.randint(key_lowest, (SEGMENTS, 1), 0, tile_count - 1)) % tile_count
    column = jnp.arange(tile_count)[None, :]
    counts = jnp.where(column == highest, most_kept, counts)
    counts = jnp.where(column == lowest, least_kept, counts)
    slot_ids = jnp.arange(most_kept)[None, None, :]
    return jnp.where(slot_ids < counts[:, :, None], orders, -1).astype(jnp.int32)


def draw_in_index(key, part):
    return mask_lists(jax.random.fold_in(key, 11), RB_OUT, RB_IN, MAXB)


def draw_out_index(key, part):
    return mask_lists(jax.random.fold_in(key, 12), RB_IN, RB_OUT, MAXO)


def level_of(rng, shape, cuts, smallest, top_value):
    loudness, own = 1.0, jax.random.fold_in(rng, 6)
    for axis_at, blocks in cuts:
        draws = jnp.exp(jax.random.uniform(jax.random.fold_in(own, axis_at), (blocks,), jnp.float32, smallest / len(cuts), top_value / len(cuts)))
        loudness = loudness * jnp.repeat(draws, shape[axis_at] // blocks).reshape([-1 if axis == axis_at else 1 for axis in range(len(shape))])
    return loudness


def centred(own_key, shape, width, limit, pieces=(), held_as=jnp.bfloat16):
    loudness = level_of(own_key, shape, pieces, -0.22, 0.18) if pieces else 1.0
    array = jax.random.normal(own_key, shape, jnp.float32) * width * loudness
    return jnp.minimum(jnp.maximum(array, -limit), limit).astype(held_as)


def setup_inputs(seed: int = 0, part: int = 0) -> dict:
    streams_of = jax.random.split(jax.random.key(seed), 8)
    part_keys = jax.random.split(jax.random.fold_in(streams_of[7], part), 8)
    return {
        "x_in": centred(part_keys[0], (TOKENS, D), 1.0, 6.0, ((1, 32),)),
        "norm_gain": jnp.clip(1.0 + 0.1 * jax.random.normal(streams_of[1], (SEGMENTS, D), jnp.float32), 0.5, 1.5),
        "in_index": draw_in_index(jax.random.fold_in(streams_of[7], 71), part),
        "gate_blocks": centred(streams_of[3], (SEGMENTS, RB_OUT, MAXB, BS * BS), (D // 2) ** -0.5, 0.09375, ((0, 4), (1, 32))),
        "up_blocks": centred(streams_of[4], (SEGMENTS, RB_OUT, MAXB, BS * BS), (D // 2) ** -0.5, 0.09375, ((0, 4), (1, 32))),
        "out_index": draw_out_index(jax.random.fold_in(streams_of[7], 71), part),
        "down_blocks": centred(streams_of[6], (SEGMENTS, RB_IN, MAXO, BS * BS), (FFW // 2) ** -0.5, 0.0625, ((0, 4), (1, 32))),
    }


def sparse_apply(left, index, blocks):
    rows = left.shape[0]
    split_rows = left.reshape(rows, -1, BS).astype(jnp.float32)

    def one_tile(pair):
        tile_index, tile_blocks = pair
        kept = (tile_index >= 0).astype(jnp.float32)
        safe_index = jnp.maximum(tile_index, 0).astype(jnp.int32)
        taken = jnp.take(split_rows, safe_index, axis=1)
        weights = tile_blocks.astype(jnp.float32).reshape(-1, BS, BS) * kept[:, None, None]
        return jnp.einsum('rmi,mij->rj', taken, weights)
    tiles = lax.map(one_tile, (index, blocks))
    return jnp.transpose(tiles, (1, 0, 2)).reshape(rows, -1)

def reference(x_in, norm_gain, in_index, gate_blocks, up_blocks, out_index, down_blocks):
    current = x_in
    results = []
    for section in range(SEGMENTS):
        wide = current.astype(jnp.float32)
        stat = lax.optimization_barrier(jnp.mean(wide * wide, axis=1, keepdims=True))
        normed = (wide * lax.rsqrt(stat + 1e-05) * norm_gain[section][None, :]).astype(jnp.bfloat16)
        gate = sparse_apply(normed, in_index[section], gate_blocks[section])
        up_part = sparse_apply(normed, in_index[section], up_blocks[section])
        hidden = (jax.nn.silu(gate) * up_part).astype(jnp.bfloat16)
        mixed = sparse_apply(hidden, out_index[section], down_blocks[section])
        current = (wide + mixed).astype(jnp.bfloat16)
        results.append(current)
    return jnp.stack(results)
```

```python
import functools

import jax
import jax.numpy as jnp
from jax import lax
from jax.experimental import pallas as pl
from jax.experimental.pallas import tpu as pltpu
from jax.sharding import PartitionSpec as P

D = 8192
FFW = 14336
BS = 64
CHIPS = 16
ROWS = 64
GU_ROWS = D // 2
GU_COLS = 14 * 128
DN_ROWS = 32 * 256
DN_COLS = 4 * 128
MIB = 1 << 20


def pack_target(kept, per_device, stride, rows):
    device = kept // per_device
    block = (device % 2) * CHIPS + device // 2
    return pl.multiple_of(
        jnp.where(kept >= 0, block * stride + (kept % per_device) * 32, rows - 32), 32
    )


def clear(target):
    rows, cols = target.shape

    def one(at, _):
        target[pl.ds(pl.multiple_of(at * 32, 32), 32), :] = jnp.zeros((32, cols), target.dtype)
        return 0

    lax.fori_loop(0, rows // 32, one, 0)


def wide_pack_kernel(index_ref, gate_hbm, up_hbm, target, buf, spread, sems):
    tiles, slots = index_ref.shape
    copies = []
    for which, source in enumerate((gate_hbm, up_hbm)):
        for tile in range(tiles):
            at = which * tiles + tile
            copies.append(pltpu.make_async_copy(source.at[tile], buf.at[at], sems.at[at]))
    for copy in copies:
        copy.start()
    clear(target)

    def place(chunk, count, first, half, tile, column):
        for part in range(32):
            spread[half, part * 16 : part * 16 + count, :] = chunk[:, part * 128 : (part + 1) * 128]
        for row in range(count):
            at = pack_target(index_ref[tile, first + row], 4, 128, target.shape[0])
            piece = spread[half, pl.ds(row, 32, stride=16), :]
            target[pl.ds(at, 32), pl.ds(column, 128)] = piece.astype(target.dtype)

    def one(at, _):
        pltpu.make_async_copy(gate_hbm.at[0], buf.at[at], sems.at[at]).wait()
        which = (at >= tiles).astype(jnp.int32)
        tile = at - which * tiles
        last = tiles - 1
        column = pl.multiple_of(jnp.where(tile == last, 2 * last + which, which * last + tile) * 128, 128)

        def pair(step, _):
            for half in range(2):
                first = pl.multiple_of(step * 32 + half * 16, 16)
                chunk = buf[at, pl.ds(first, 16), :].astype(jnp.float32)
                place(chunk, 16, first, half, tile, column)
            return 0

        lax.fori_loop(0, slots // 32, pair, 0)
        done = slots // 32 * 32
        half = 0
        while done < slots:
            count = min(16, slots - done)
            chunk = buf[at, done : done + count, :].astype(jnp.float32)
            place(chunk, count, done, half, tile, column)
            done += count
            half = 1 - half
        return 0

    lax.fori_loop(0, 2 * tiles, one, 0)


def down_pack_kernel(index_ref, source, target, buf, spread, sems):
    tiles, slots = index_ref.shape
    parts = 7
    size = slots // parts
    copies = [
        pltpu.make_async_copy(
            source.at[pl.ds(part * size, size)], buf.at[pl.ds(part * size, size)], sems.at[part]
        )
        for part in range(parts)
    ]
    for copy in copies:
        copy.start()
    clear(target)
    def one(part, _):
        pltpu.make_async_copy(
            source.at[pl.ds(0, size)], buf.at[pl.ds(part * size, size)], sems.at[part]
        ).wait()

        def step(at, _):
            for half in range(2):
                slot = part * size + at * 6 + half * 3
                for inner in range(3):
                    chunk = buf[slot + inner].astype(jnp.float32)
                    for lane in range(32):
                        spread[half, lane * 16 + inner * 4 : lane * 16 + inner * 4 + 4, :] = chunk[
                            :, lane * 128 : (lane + 1) * 128
                        ]
                for inner in range(3):
                    for tile in range(tiles):
                        goal = pack_target(index_ref[tile, slot + inner], 7, 256, target.shape[0])
                        piece = spread[half, pl.ds(inner * 4 + tile, 32, stride=16), :]
                        target[pl.ds(goal, 32), tile * 128 : (tile + 1) * 128] = piece.astype(target.dtype)
            return 0

        lax.fori_loop(0, size // 6, step, 0)
        return 0

    lax.fori_loop(0, parts, one, 0)


def pack(kernel, index, sources, buf, copies, shape, name):
    sources = [pltpu.with_memory_space_constraint(source, pltpu.HBM) for source in sources]
    return pl.pallas_call(
        kernel,
        out_shape=pltpu.VMEM(shape, jnp.bfloat16),
        in_specs=[pl.BlockSpec(memory_space=pltpu.SMEM)]
        + [pl.BlockSpec(memory_space=pltpu.HBM)] * len(sources),
        out_specs=pl.BlockSpec(memory_space=pltpu.VMEM),
        scratch_shapes=[
            pltpu.VMEM(buf, jnp.bfloat16),
            pltpu.VMEM((2, 32 * 16, 128), jnp.float32),
            pltpu.SemaphoreType.DMA((copies,)),
        ],
        compiler_params=pltpu.CompilerParams(vmem_limit_bytes=12 * MIB),
        cost_estimate=pl.CostEstimate(flops=0, bytes_accessed=40 * MIB, transcendentals=0),
        name=name,
    )(index, *sources)


def densify_wide(index, gate_blocks, up_blocks):
    tiles, slots = index.shape
    buf = (2 * tiles, slots, BS * BS)
    shape = (GU_ROWS + 32, GU_COLS)
    return pack(wide_pack_kernel, index, (gate_blocks, up_blocks), buf, 2 * tiles, shape, "pack_wide")


def densify_down(index, blocks):
    tiles, slots = index.shape
    shape = (DN_ROWS + 32, DN_COLS)
    blocks = jnp.transpose(blocks, (1, 0, 2))
    return pack(down_pack_kernel, index, (blocks,), (slots, tiles, BS * BS), 7, shape, "pack_down")


def densify(in_index, gate_blocks, up_blocks, out_index, down_blocks):
    return densify_wide(in_index, gate_blocks, up_blocks), densify_down(out_index, down_blocks)


def fold(even, odd, at):
    low = lax.broadcasted_iota(jnp.int32, (ROWS, 128), 1) < 64
    e0, e1 = even[:, at : at + 128], even[:, at + 128 : at + 256]
    o0, o1 = odd[:, at : at + 128], odd[:, at + 128 : at + 256]
    return jnp.where(low, e0, o1) + pltpu.roll(jnp.where(low, e1, o0), 64, 1)


def wide_kernel(core_ref, mine_ref, other_ref, gain_ref, weight_ref, order_ref, out_ref, normed):
    core = core_ref[0]
    total = jnp.zeros((2 * ROWS, 128), jnp.float32)
    for ref in (mine_ref, other_ref):
        for chip in range(CHIPS):
            value = ref[chip].astype(jnp.float32)
            total += value * value
    stat = jnp.sum(total[:ROWS] + total[ROWS:], axis=1, keepdims=True) / D
    scale = lax.rsqrt(stat + 1e-05)
    scale = jnp.concatenate([scale, scale], axis=0)
    starts = (core, 1 - core)
    for which, ref in enumerate((mine_ref, other_ref)):
        gains = gain_ref[pl.ds(pl.multiple_of(starts[which] * 32, 32), 32), :]
        for chip in range(CHIPS):
            gain = jnp.concatenate(
                [
                    jnp.broadcast_to(gains[2 * chip : 2 * chip + 1], (ROWS, 128)),
                    jnp.broadcast_to(gains[2 * chip + 1 : 2 * chip + 2], (ROWS, 128)),
                ],
                axis=0,
            )
            value = ref[chip].astype(jnp.float32) * scale * gain
            normed[which, :, chip * 128 : (chip + 1) * 128] = value.astype(jnp.bfloat16)

    def product(tile):
        acc = None
        for which in range(2):
            rows = pl.ds(pl.multiple_of(starts[which] * (GU_ROWS // 2), GU_ROWS // 2), GU_ROWS // 2)
            part = jnp.dot(
                normed[which],
                weight_ref[rows, tile * 256 : (tile + 1) * 256],
                preferred_element_type=jnp.float32,
            )
            acc = part if acc is None else acc + part
        return fold(acc[:ROWS], acc[ROWS:], 0)

    pieces = []
    for pair in range(3):
        gate = product(pair)
        up = product(pair + 3)
        pieces.append((gate / (1.0 + jnp.exp(-gate)) * up).astype(jnp.bfloat16))
    both = product(6)
    last = both / (1.0 + jnp.exp(-both)) * pltpu.roll(both, 64, 1)
    low = lax.broadcasted_iota(jnp.int32, (ROWS, 128), 1) < 64
    pieces.append(jnp.where(low, last, 0.0).astype(jnp.bfloat16))
    hidden = jnp.dot(
        jnp.concatenate(pieces, axis=1), order_ref[...], preferred_element_type=jnp.float32
    ).astype(jnp.bfloat16)
    hidden = jnp.concatenate([hidden[:, :256], hidden[:, 256:]], axis=0)
    for chip in range(CHIPS):
        out_ref[chip] = hidden


def down_kernel(core_ref, mine_ref, other_ref, weight_ref, taken_ref, order_ref, back_ref, out_ref, next_ref):
    core = core_ref[0]
    acc = None
    for ref, start in ((mine_ref, core), (other_ref, 1 - core)):
        rows = pl.ds(pl.multiple_of(start * (DN_ROWS // 2), DN_ROWS // 2), DN_ROWS // 2)
        left = jnp.concatenate([ref[chip] for chip in range(CHIPS)], axis=1)
        part = jnp.dot(left, weight_ref[rows, :], preferred_element_type=jnp.float32)
        acc = part if acc is None else acc + part
    even, odd = acc[:ROWS], acc[ROWS:]
    mixed = jnp.concatenate([fold(even, odd, 0), fold(even, odd, 256)], axis=1)
    taken = jnp.concatenate([taken_ref[:ROWS], taken_ref[ROWS:]], axis=1)
    taken = jnp.dot(taken, back_ref[...], preferred_element_type=jnp.float32)
    produced = (taken + mixed).astype(jnp.bfloat16)
    out_ref[...] = produced
    ordered = jnp.dot(produced, order_ref[...], preferred_element_type=jnp.float32).astype(jnp.bfloat16)
    next_ref[...] = jnp.concatenate([ordered[:, :128], ordered[:, 128:]], axis=0)


def call_wide(core, mine, other, gain, weight, order):
    vmem = pl.BlockSpec(memory_space=pltpu.VMEM)
    return pl.pallas_call(
        wide_kernel,
        out_shape=jax.ShapeDtypeStruct((CHIPS, 2 * ROWS, 256), jnp.bfloat16),
        in_specs=[pl.BlockSpec(memory_space=pltpu.SMEM)] + [vmem] * 5,
        out_specs=vmem,
        scratch_shapes=[pltpu.VMEM((2, 2 * ROWS, GU_ROWS // 2), jnp.bfloat16)],
        compiler_params=pltpu.CompilerParams(vmem_limit_bytes=24 * MIB),
        cost_estimate=pl.CostEstimate(flops=2 * 128 * GU_ROWS * GU_COLS, bytes_accessed=2 * MIB, transcendentals=0),
        name="wide",
    )(core, mine, other, gain, pltpu.with_memory_space_constraint(weight, pltpu.VMEM), order)


def call_down(core, mine, other, weight, taken, order, back):
    vmem = pl.BlockSpec(memory_space=pltpu.VMEM)
    return pl.pallas_call(
        down_kernel,
        out_shape=(
            jax.ShapeDtypeStruct((ROWS, 256), jnp.bfloat16),
            jax.ShapeDtypeStruct((2 * ROWS, 128), jnp.bfloat16),
        ),
        in_specs=[pl.BlockSpec(memory_space=pltpu.SMEM)] + [vmem] * 6,
        out_specs=(vmem, vmem),
        compiler_params=pltpu.CompilerParams(vmem_limit_bytes=24 * MIB),
        cost_estimate=pl.CostEstimate(flops=2 * 128 * DN_ROWS * DN_COLS, bytes_accessed=2 * MIB, transcendentals=0),
        name="down",
    )(core, mine, other, pltpu.with_memory_space_constraint(weight, pltpu.VMEM), taken, order, back)


def orders():
    source = jnp.arange(256)
    goal = (source % 2) * 128 + source // 64 * 32 + source % 64 // 2
    x_order = (goal[:, None] == jnp.arange(256)[None, :]).astype(jnp.bfloat16)
    source = jnp.arange(512)
    goal = (source % 2) * 256 + source // 64 * 32 + source % 64 // 2
    h_order = (goal[:, None] == jnp.arange(512)[None, :]).astype(jnp.bfloat16)
    return x_order, h_order


def gathered(value):
    same_core = [[2 * chip + core for chip in range(CHIPS)] for core in range(2)]
    mine = lax.all_to_all(value, "tensor", 0, 0, axis_index_groups=same_core)
    swap = [(i, i ^ 1) for i in range(2 * CHIPS)]
    return mine, lax.ppermute(mine, "tensor", swap)


def local(x_in, norm_gain, in_index, gate_blocks, up_blocks, out_index, down_blocks):
    segment_count = lax.axis_size("segment")
    segment_at = lax.axis_index("segment")
    core = (lax.axis_index("tensor") % 2).astype(jnp.int32)[None]
    tokens = x_in.shape[0]
    group_count = tokens // ROWS
    tick_count = group_count + segment_count - 1
    x_order, h_order = orders()
    x_back = x_order.T
    gain = jnp.dot(
        norm_gain[0].reshape(2 * CHIPS, 256), x_order.astype(jnp.float32), precision=lax.Precision.HIGHEST
    )
    gain = gain.reshape(CHIPS, 2, 2, 128).transpose(1, 0, 2, 3).reshape(4 * CHIPS, 128)
    x_ordered = jnp.dot(x_in, x_order, preferred_element_type=jnp.float32).astype(jnp.bfloat16)
    firsts = []
    for group in range(group_count):
        part = x_ordered[group * ROWS : (group + 1) * ROWS]
        firsts.append(jnp.concatenate([part[:, :128], part[:, 128:]], axis=0))
    here = [jnp.broadcast_to(segment_at == segment, (8, 128)).astype(jnp.bfloat16) for segment in range(segment_count)]
    in_index, out_index = in_index[0], out_index[0]
    in_index, out_index, core, x_order, x_back, h_order, gain, firsts, here = lax.optimization_barrier(
        (in_index, out_index, core, x_order, x_back, h_order, gain, firsts, here)
    )
    wide = densify_wide(in_index, gate_blocks[0], up_blocks[0])
    down = densify_down(out_index, down_blocks[0])
    firsts, wide, down = lax.optimization_barrier((firsts, wide, down))

    def is_here(segment, shape):
        return jnp.tile(here[segment], (shape[0] // 8, shape[1] // 128)) > 0

    carried = None
    made = []
    hops = [(i, i + 1) for i in range(segment_count - 1)]
    for tick in range(tick_count):
        taken = firsts[min(tick, group_count - 1)]
        if carried is not None:
            taken = jnp.where(is_here(0, taken.shape), taken, carried)
        mine, other = gathered(jnp.broadcast_to(taken[None], (CHIPS, 2 * ROWS, 128)))
        hidden = call_wide(core, mine, other, gain, wide, h_order)
        mine, other = gathered(hidden)
        produced, ordered = call_down(core, mine, other, down, taken, x_order, x_back)
        made.append(produced)
        if tick + 1 < tick_count:
            carried = lax.ppermute(ordered, "segment", hops)
    groups = []
    for group in range(group_count):
        chosen = made[group]
        for segment in range(1, segment_count):
            chosen = jnp.where(is_here(segment, chosen.shape), made[group + segment], chosen)
        groups.append(chosen)
    return jnp.concatenate(groups, axis=0)[None]


def solution(mesh):
    placed = (
        P("replica", "tensor"),
        P("segment", None),
        P("segment", "tensor", None),
        P("segment", "tensor", None, None),
        P("segment", "tensor", None, None),
        P("segment", "tensor", None),
        P("segment", "tensor", None, None),
    )
    return jax.shard_map(
        local,
        mesh=mesh,
        in_specs=placed,
        out_specs=P("segment", "replica", "tensor"),
        check_vma=False,
    )
```

```python
import functools

import jax
import jax.numpy as jnp
from jax import lax
from jax.experimental import pallas as pl
from jax.experimental.pallas import tpu as pltpu
from jax.sharding import PartitionSpec as P

D = 8192
FFW = 14336
BS = 64
CHIPS = 16
ROWS = 64
GU_ROWS = D // 2
GU_COLS = 14 * 128
DN_ROWS = 32 * 256
DN_COLS = 4 * 128
MIB = 1 << 20


def targets(index, per_device, stride, rows):
    device = index // per_device
    block = (device % 2) * CHIPS + device // 2
    return jnp.where(index >= 0, block * stride + (index % per_device) * 32, rows - 32)


def clear(target):
    rows, cols = target.shape

    def one(at, _):
        target[pl.ds(pl.multiple_of(at * 32, 32), 32), :] = jnp.zeros((32, cols), target.dtype)
        return 0

    lax.fori_loop(0, rows // 32, one, 0)


def wide_pack_kernel(goal_ref, gate_hbm, up_hbm, target, buf, spread, sems):
    tiles, slots = goal_ref.shape
    for which, source in enumerate((gate_hbm, up_hbm)):
        for tile in range(tiles):
            at = which * tiles + tile
            pltpu.make_async_copy(source.at[tile], buf.at[at], sems.at[at]).start()
    clear(target)

    def place(chunk, count, first, half, tile, column):
        for group in range(0, count, 8):
            for part in range(32):
                spread[half, group * 32 + part * 8 : group * 32 + part * 8 + 8, :] = chunk[
                    group : group + 8, part * 128 : (part + 1) * 128
                ]
        for row in range(count):
            goal = pl.multiple_of(goal_ref[tile, first + row], 32)
            piece = spread[half, pl.ds(row // 8 * 256 + row % 8, 32, stride=8), :]
            target[pl.ds(goal, 32), pl.ds(column, 128)] = piece.astype(target.dtype)

    def one(at, _):
        pltpu.make_async_copy(gate_hbm.at[0], buf.at[at], sems.at[at]).wait()
        which = (at >= tiles).astype(jnp.int32)
        tile = at - which * tiles
        last = tiles - 1
        column = pl.multiple_of(jnp.where(tile == last, 2 * last + which, which * last + tile) * 128, 128)

        def pair(step, _):
            for half in range(2):
                first = pl.multiple_of(step * 32 + half * 16, 16)
                chunk = buf[at, pl.ds(first, 16), :].astype(jnp.float32)
                place(chunk, 16, first, half, tile, column)
            return 0

        lax.fori_loop(0, slots // 32, pair, 0)
        done = slots // 32 * 32
        half = 0
        while done < slots:
            count = min(16, slots - done)
            chunk = buf[at, done : done + count, :].astype(jnp.float32)
            place(chunk, count, done, half, tile, column)
            done += count
            half = 1 - half
        return 0

    lax.fori_loop(0, 2 * tiles, one, 0)


def down_pack_kernel(goal_ref, source, target, buf, spread, sems):
    tiles, slots = goal_ref.shape
    parts = 7
    size = slots // parts
    for part in range(parts):
        pltpu.make_async_copy(
            source.at[pl.ds(part * size, size)], buf.at[pl.ds(part * size, size)], sems.at[part]
        ).start()
    clear(target)

    def one(part, _):
        pltpu.make_async_copy(
            source.at[pl.ds(0, size)], buf.at[pl.ds(part * size, size)], sems.at[part]
        ).wait()

        def step(at, _):
            for half in range(3):
                slot = part * size + at * 6 + half * 2
                for inner in range(2):
                    chunk = buf[slot + inner].astype(jnp.float32)
                    for lane in range(32):
                        spread[half, lane * 8 + inner * 4 : lane * 8 + inner * 4 + 4, :] = chunk[
                            :, lane * 128 : (lane + 1) * 128
                        ]
                for inner in range(2):
                    for tile in range(tiles):
                        goal = pl.multiple_of(goal_ref[tile, slot + inner], 32)
                        piece = spread[half, pl.ds(inner * 4 + tile, 32, stride=8), :]
                        target[pl.ds(goal, 32), tile * 128 : (tile + 1) * 128] = piece.astype(target.dtype)
            return 0

        lax.fori_loop(0, size // 6, step, 0)
        return 0

    lax.fori_loop(0, parts, one, 0)


def pack(kernel, goals, sources, buf, spread, copies, shape, name):
    sources = [pltpu.with_memory_space_constraint(source, pltpu.HBM) for source in sources]
    return pl.pallas_call(
        kernel,
        out_shape=pltpu.VMEM(shape, jnp.bfloat16),
        in_specs=[pl.BlockSpec(memory_space=pltpu.SMEM)]
        + [pl.BlockSpec(memory_space=pltpu.HBM)] * len(sources),
        out_specs=pl.BlockSpec(memory_space=pltpu.VMEM),
        scratch_shapes=[
            pltpu.VMEM(buf, jnp.bfloat16),
            pltpu.VMEM(spread + (128,), jnp.float32),
            pltpu.SemaphoreType.DMA((copies,)),
        ],
        compiler_params=pltpu.CompilerParams(vmem_limit_bytes=12 * MIB),
        cost_estimate=pl.CostEstimate(flops=0, bytes_accessed=40 * MIB, transcendentals=0),
        name=name,
    )(goals, *sources)


def densify_wide(goals, gate_blocks, up_blocks):
    tiles, slots = goals.shape
    buf = (2 * tiles, slots, BS * BS)
    shape = (GU_ROWS + 32, GU_COLS)
    sources = (gate_blocks, up_blocks)
    return pack(wide_pack_kernel, goals, sources, buf, (2, 512), 2 * tiles, shape, "pack_wide")


def densify_down(goals, blocks):
    tiles, slots = goals.shape
    shape = (DN_ROWS + 32, DN_COLS)
    blocks = jnp.transpose(blocks, (1, 0, 2))
    return pack(down_pack_kernel, goals, (blocks,), (slots, tiles, BS * BS), (3, 256), 7, shape, "pack_down")


def in_goals(index):
    return targets(index, 4, 128, GU_ROWS + 32)


def out_goals(index):
    return targets(index, 7, 256, DN_ROWS + 32)


def densify(in_index, gate_blocks, up_blocks, out_index, down_blocks):
    return (
        densify_wide(in_goals(in_index), gate_blocks, up_blocks),
        densify_down(out_goals(out_index), down_blocks),
    )


def fold(even, odd, at):
    low = lax.broadcasted_iota(jnp.int32, (ROWS, 128), 1) < 64
    e0, e1 = even[:, at : at + 128], even[:, at + 128 : at + 256]
    o0, o1 = odd[:, at : at + 128], odd[:, at + 128 : at + 256]
    return jnp.where(low, e0, o1) + pltpu.roll(jnp.where(low, e1, o0), 64, 1)


def wide_kernel(core_ref, mine_ref, other_ref, gain_ref, weight_ref, order_ref, out_ref, normed):
    core = core_ref[0]
    total = jnp.zeros((2 * ROWS, 128), jnp.float32)
    for ref in (mine_ref, other_ref):
        for chip in range(CHIPS):
            value = ref[chip].astype(jnp.float32)
            total += value * value
    stat = jnp.sum(total[:ROWS] + total[ROWS:], axis=1, keepdims=True) / D
    scale = lax.rsqrt(stat + 1e-05)
    scale = jnp.concatenate([scale, scale], axis=0)
    starts = (core, 1 - core)
    for which, ref in enumerate((mine_ref, other_ref)):
        gains = gain_ref[pl.ds(pl.multiple_of(starts[which] * 32, 32), 32), :]
        for chip in range(CHIPS):
            gain = jnp.concatenate(
                [
                    jnp.broadcast_to(gains[2 * chip : 2 * chip + 1], (ROWS, 128)),
                    jnp.broadcast_to(gains[2 * chip + 1 : 2 * chip + 2], (ROWS, 128)),
                ],
                axis=0,
            )
            value = ref[chip].astype(jnp.float32) * scale * gain
            normed[which, :, chip * 128 : (chip + 1) * 128] = value.astype(jnp.bfloat16)

    def product(tile):
        acc = None
        for which in range(2):
            rows = pl.ds(pl.multiple_of(starts[which] * (GU_ROWS // 2), GU_ROWS // 2), GU_ROWS // 2)
            part = jnp.dot(
                normed[which],
                weight_ref[rows, tile * 256 : (tile + 1) * 256],
                preferred_element_type=jnp.float32,
            )
            acc = part if acc is None else acc + part
        return fold(acc[:ROWS], acc[ROWS:], 0)

    pieces = []
    for pair in range(3):
        gate = product(pair)
        up = product(pair + 3)
        pieces.append((gate / (1.0 + jnp.exp(-gate)) * up).astype(jnp.bfloat16))
    both = product(6)
    last = both / (1.0 + jnp.exp(-both)) * pltpu.roll(both, 64, 1)
    low = lax.broadcasted_iota(jnp.int32, (ROWS, 128), 1) < 64
    pieces.append(jnp.where(low, last, 0.0).astype(jnp.bfloat16))
    hidden = jnp.dot(
        jnp.concatenate(pieces, axis=1), order_ref[...], preferred_element_type=jnp.float32
    ).astype(jnp.bfloat16)
    hidden = jnp.concatenate([hidden[:, :256], hidden[:, 256:]], axis=0)
    for chip in range(CHIPS):
        out_ref[chip] = hidden


def down_kernel(core_ref, mine_ref, other_ref, weight_ref, taken_ref, order_ref, back_ref, out_ref, next_ref):
    core = core_ref[0]
    acc = None
    for ref, start in ((mine_ref, core), (other_ref, 1 - core)):
        rows = pl.ds(pl.multiple_of(start * (DN_ROWS // 2), DN_ROWS // 2), DN_ROWS // 2)
        left = jnp.concatenate([ref[chip] for chip in range(CHIPS)], axis=1)
        part = jnp.dot(left, weight_ref[rows, :], preferred_element_type=jnp.float32)
        acc = part if acc is None else acc + part
    even, odd = acc[:ROWS], acc[ROWS:]
    mixed = jnp.concatenate([fold(even, odd, 0), fold(even, odd, 256)], axis=1)
    taken = jnp.concatenate([taken_ref[:ROWS], taken_ref[ROWS:]], axis=1)
    taken = jnp.dot(taken, back_ref[...], preferred_element_type=jnp.float32)
    produced = (taken + mixed).astype(jnp.bfloat16)
    out_ref[...] = produced
    ordered = jnp.dot(produced, order_ref[...], preferred_element_type=jnp.float32).astype(jnp.bfloat16)
    next_ref[...] = jnp.concatenate([ordered[:, :128], ordered[:, 128:]], axis=0)


def call_wide(core, mine, other, gain, weight, order):
    vmem = pl.BlockSpec(memory_space=pltpu.VMEM)
    return pl.pallas_call(
        wide_kernel,
        out_shape=jax.ShapeDtypeStruct((CHIPS, 2 * ROWS, 256), jnp.bfloat16),
        in_specs=[pl.BlockSpec(memory_space=pltpu.SMEM)] + [vmem] * 5,
        out_specs=vmem,
        scratch_shapes=[pltpu.VMEM((2, 2 * ROWS, GU_ROWS // 2), jnp.bfloat16)],
        compiler_params=pltpu.CompilerParams(vmem_limit_bytes=24 * MIB),
        cost_estimate=pl.CostEstimate(flops=2 * 128 * GU_ROWS * GU_COLS, bytes_accessed=2 * MIB, transcendentals=0),
        name="wide",
    )(core, mine, other, gain, pltpu.with_memory_space_constraint(weight, pltpu.VMEM), order)


def call_down(core, mine, other, weight, taken, order, back):
    vmem = pl.BlockSpec(memory_space=pltpu.VMEM)
    return pl.pallas_call(
        down_kernel,
        out_shape=(
            jax.ShapeDtypeStruct((ROWS, 256), jnp.bfloat16),
            jax.ShapeDtypeStruct((2 * ROWS, 128), jnp.bfloat16),
        ),
        in_specs=[pl.BlockSpec(memory_space=pltpu.SMEM)] + [vmem] * 6,
        out_specs=(vmem, vmem),
        compiler_params=pltpu.CompilerParams(vmem_limit_bytes=24 * MIB),
        cost_estimate=pl.CostEstimate(flops=2 * 128 * DN_ROWS * DN_COLS, bytes_accessed=2 * MIB, transcendentals=0),
        name="down",
    )(core, mine, other, pltpu.with_memory_space_constraint(weight, pltpu.VMEM), taken, order, back)


def orders():
    source = jnp.arange(256)
    goal = (source % 2) * 128 + source // 64 * 32 + source % 64 // 2
    x_order = (goal[:, None] == jnp.arange(256)[None, :]).astype(jnp.bfloat16)
    source = jnp.arange(512)
    goal = (source % 2) * 256 + source // 64 * 32 + source % 64 // 2
    h_order = (goal[:, None] == jnp.arange(512)[None, :]).astype(jnp.bfloat16)
    return x_order, h_order


def exchanged(value):
    same_core = [[2 * chip + core for chip in range(CHIPS)] for core in range(2)]
    return lax.all_to_all(value, "tensor", 0, 0, axis_index_groups=same_core)


def swapped(value):
    return lax.ppermute(value, "tensor", [(i, i ^ 1) for i in range(2 * CHIPS)])


def local(x_in, norm_gain, in_index, gate_blocks, up_blocks, out_index, down_blocks):
    segment_count = lax.axis_size("segment")
    segment_at = lax.axis_index("segment")
    core = (lax.axis_index("tensor") % 2).astype(jnp.int32)[None]
    tokens = x_in.shape[0]
    group_count = tokens // ROWS
    tick_count = group_count + segment_count - 1
    x_order, h_order = orders()
    x_back = x_order.T
    gain = jnp.dot(
        norm_gain.reshape(2 * CHIPS, 256), x_order.astype(jnp.float32), precision=lax.Precision.HIGHEST
    )
    gain = gain.reshape(CHIPS, 2, 2, 128).transpose(1, 0, 2, 3).reshape(4 * CHIPS, 128)
    x_ordered = jnp.dot(x_in, x_order, preferred_element_type=jnp.float32).astype(jnp.bfloat16)
    firsts = []
    for group in range(group_count):
        part = x_ordered[group * ROWS : (group + 1) * ROWS]
        firsts.append(jnp.concatenate([part[:, :128], part[:, 128:]], axis=0))
    here = [jnp.broadcast_to(segment_at == segment, (8, 128)).astype(jnp.bfloat16) for segment in range(segment_count)]
    to_wide, to_down = in_goals(in_index[0]), out_goals(out_index[0])
    to_wide, to_down, core, x_order, x_back, h_order, gain, firsts, here = lax.optimization_barrier(
        (to_wide, to_down, core, x_order, x_back, h_order, gain, firsts, here)
    )

    def is_here(segment, shape):
        return jnp.tile(here[segment], (shape[0] // 8, shape[1] // 128)) > 0

    carried = None
    made = []
    hops = [(i, i + 1) for i in range(segment_count - 1)]
    for tick in range(tick_count):
        taken = firsts[min(tick, group_count - 1)]
        if carried is not None:
            taken = jnp.where(is_here(0, taken.shape), taken, carried)
        mine = exchanged(jnp.broadcast_to(taken[None], (CHIPS, 2 * ROWS, 128)))
        if tick == 0:
            mine, to_wide = lax.optimization_barrier((mine, to_wide))
            wide = densify_wide(to_wide, gate_blocks[0], up_blocks[0])
        other = swapped(mine)
        hidden = call_wide(core, mine, other, gain, wide, h_order)
        mine = exchanged(hidden)
        if tick == 0:
            mine, to_down = lax.optimization_barrier((mine, to_down))
            down = densify_down(to_down, down_blocks[0])
        other = swapped(mine)
        produced, ordered = call_down(core, mine, other, down, taken, x_order, x_back)
        made.append(produced)
        if tick + 1 < tick_count:
            carried = lax.ppermute(ordered, "segment", hops)
    groups = []
    for group in range(group_count):
        chosen = made[group]
        for segment in range(1, segment_count):
            chosen = jnp.where(is_here(segment, chosen.shape), made[group + segment], chosen)
        groups.append(chosen)
    return jnp.concatenate(groups, axis=0)[None]


def solution(mesh):
    placed = (
        P("replica", "tensor"),
        P("segment", None),
        P("segment", "tensor", None),
        P("segment", "tensor", None, None),
        P("segment", "tensor", None, None),
        P("segment", "tensor", None),
        P("segment", "tensor", None, None),
    )
    return jax.shard_map(
        local,
        mesh=mesh,
        in_specs=placed,
        out_specs=P("segment", "replica", "tensor"),
        check_vma=False,
    )
```

```python
import functools

import jax
import jax.numpy as jnp
from jax import lax
from jax.experimental import pallas as pl
from jax.experimental.pallas import tpu as pltpu
from jax.sharding import PartitionSpec as P

D = 8192
FFW = 14336
BS = 64
CHIPS = 16
ROWS = 64
GU_ROWS = D // 2
GU_COLS = 14 * 128
DN_ROWS = 32 * 256
DN_COLS = 4 * 128
MIB = 1 << 20


def clear(target):
    rows, cols = target.shape

    def one(at, _):
        target[pl.ds(pl.multiple_of(at * 32, 32), 32), :] = jnp.zeros((32, cols), target.dtype)
        return 0

    lax.fori_loop(0, rows // 32, one, 0)


def wide_pack_kernel(goal_ref, gate_hbm, up_hbm, target, buf, spread, sems):
    tiles, slots = goal_ref.shape
    for which, source in enumerate((gate_hbm, up_hbm)):
        for tile in range(tiles):
            at = which * tiles + tile
            pltpu.make_async_copy(source.at[tile], buf.at[at], sems.at[at]).start()
    clear(target)

    def place(chunk, count, first, half, tile, column):
        for group in range(0, count, 8):
            for part in range(32):
                spread[half, group * 32 + part * 8 : group * 32 + part * 8 + 8, :] = chunk[
                    group : group + 8, part * 128 : (part + 1) * 128
                ]
        for row in range(count):
            goal = pl.multiple_of(goal_ref[tile, first + row], 32)
            piece = spread[half, pl.ds(row // 8 * 256 + row % 8, 32, stride=8), :]
            target[pl.ds(goal, 32), pl.ds(column, 128)] = piece.astype(target.dtype)

    def one(at, _):
        pltpu.make_async_copy(gate_hbm.at[0], buf.at[at], sems.at[at]).wait()
        which = (at >= tiles).astype(jnp.int32)
        tile = at - which * tiles
        last = tiles - 1
        column = pl.multiple_of(jnp.where(tile == last, 2 * last + which, which * last + tile) * 128, 128)

        def pair(step, _):
            for half in range(2):
                first = pl.multiple_of(step * 32 + half * 16, 16)
                chunk = buf[at, pl.ds(first, 16), :].astype(jnp.float32)
                place(chunk, 16, first, half, tile, column)
            return 0

        lax.fori_loop(0, slots // 32, pair, 0)
        done = slots // 32 * 32
        half = 0
        while done < slots:
            count = min(16, slots - done)
            chunk = buf[at, done : done + count, :].astype(jnp.float32)
            place(chunk, count, done, half, tile, column)
            done += count
            half = 1 - half
        return 0

    lax.fori_loop(0, 2 * tiles, one, 0)


def down_pack_kernel(goal_ref, source, near, far, buf, spread, sems):
    tiles, slots = goal_ref.shape[0] // 2, goal_ref.shape[1]
    parts = 7
    size = slots // parts
    for part in range(parts):
        pltpu.make_async_copy(
            source.at[pl.ds(part * size, size)], buf.at[pl.ds(part * size, size)], sems.at[part]
        ).start()
    clear(near)
    clear(far)

    def one(part, _):
        pltpu.make_async_copy(
            source.at[pl.ds(0, size)], buf.at[pl.ds(part * size, size)], sems.at[part]
        ).wait()

        def step(at, _):
            for half in range(3):
                slot = part * size + at * 6 + half * 2
                for inner in range(2):
                    chunk = buf[slot + inner].astype(jnp.float32)
                    for lane in range(32):
                        spread[half, lane * 8 + inner * 4 : lane * 8 + inner * 4 + 4, :] = chunk[
                            :, lane * 128 : (lane + 1) * 128
                        ]
                for inner in range(2):
                    for tile in range(tiles):
                        piece = spread[half, pl.ds(inner * 4 + tile, 32, stride=8), :].astype(near.dtype)
                        for which, target in enumerate((near, far)):
                            goal = pl.multiple_of(goal_ref[which * tiles + tile, slot + inner], 32)
                            target[pl.ds(goal, 32), tile * 128 : (tile + 1) * 128] = piece
            return 0

        lax.fori_loop(0, size // 6, step, 0)
        return 0

    lax.fori_loop(0, parts, one, 0)


def pack(kernel, goals, sources, buf, spread, copies, shape, results, name):
    sources = [pltpu.with_memory_space_constraint(source, pltpu.HBM) for source in sources]
    return pl.pallas_call(
        kernel,
        out_shape=[pltpu.VMEM(shape, jnp.bfloat16)] * results,
        in_specs=[pl.BlockSpec(memory_space=pltpu.SMEM)]
        + [pl.BlockSpec(memory_space=pltpu.HBM)] * len(sources),
        out_specs=[pl.BlockSpec(memory_space=pltpu.VMEM)] * results,
        scratch_shapes=[
            pltpu.VMEM(buf, jnp.bfloat16),
            pltpu.VMEM(spread + (128,), jnp.float32),
            pltpu.SemaphoreType.DMA((copies,)),
        ],
        compiler_params=pltpu.CompilerParams(vmem_limit_bytes=12 * MIB),
        cost_estimate=pl.CostEstimate(flops=0, bytes_accessed=40 * MIB, transcendentals=0),
        name=name,
    )(goals, *sources)


def densify_wide(goals, gate_blocks, up_blocks):
    tiles, slots = goals.shape
    buf = (2 * tiles, slots, BS * BS)
    shape = (GU_ROWS + 32, GU_COLS)
    sources = (gate_blocks, up_blocks)
    return pack(wide_pack_kernel, goals, sources, buf, (2, 512), 2 * tiles, shape, 1, "pack_wide")[0]


def densify_down(goals, blocks):
    tiles, slots = blocks.shape[:2]
    shape = (DN_ROWS // 2 + 32, DN_COLS)
    blocks = jnp.transpose(blocks, (1, 0, 2))
    buf = (slots, tiles, BS * BS)
    return pack(down_pack_kernel, goals, (blocks,), buf, (3, 256), 7, shape, 2, "pack_down")


def in_goals(index):
    device = index // 4
    row = ((device % 2) * CHIPS + device // 2) * 128 + (index % 4) * 32
    return jnp.where(index >= 0, row, GU_ROWS)


def out_goals(index, core):
    device = index // 7
    row = device // 2 * 256 + (index % 7) * 32
    near = (device % 2) == core
    trash = DN_ROWS // 2
    return jnp.concatenate(
        [
            jnp.where((index >= 0) & near, row, trash),
            jnp.where((index >= 0) & jnp.logical_not(near), row, trash),
        ],
        axis=0,
    )


def fold(even, odd, at):
    low = lax.broadcasted_iota(jnp.int32, (ROWS, 128), 1) < 64
    e0, e1 = even[:, at : at + 128], even[:, at + 128 : at + 256]
    o0, o1 = odd[:, at : at + 128], odd[:, at + 128 : at + 256]
    return jnp.where(low, e0, o1) + pltpu.roll(jnp.where(low, e1, o0), 64, 1)


def near_kernel(core_ref, part_ref, gain_ref, weight_ref, acc_ref, square_ref, scaled):
    core = core_ref[0]
    total = jnp.zeros((2 * ROWS, 128), jnp.float32)
    gains = gain_ref[pl.ds(pl.multiple_of(core * 32, 32), 32), :]
    for chip in range(CHIPS):
        value = part_ref[chip].astype(jnp.float32)
        total += value * value
        scaled[:, chip * 128 : (chip + 1) * 128] = (value * both_rows(gains, chip)).astype(jnp.bfloat16)
    square_ref[...] = total
    rows = pl.ds(pl.multiple_of(core * (GU_ROWS // 2), GU_ROWS // 2), GU_ROWS // 2)
    for tile in range(7):
        acc_ref[:, tile * 256 : (tile + 1) * 256] = jnp.dot(
            scaled[...], weight_ref[rows, tile * 256 : (tile + 1) * 256], preferred_element_type=jnp.float32
        )


def both_rows(gains, chip):
    return jnp.concatenate(
        [jnp.broadcast_to(gains[2 * chip + p : 2 * chip + p + 1], (ROWS, 128)) for p in range(2)], axis=0
    )


def far_kernel(core_ref, part_ref, gain_ref, weight_ref, order_ref, acc_ref, square_ref, out_ref, scaled):
    core = 1 - core_ref[0]
    total = square_ref[...]
    gains = gain_ref[pl.ds(pl.multiple_of(core * 32, 32), 32), :]
    for chip in range(CHIPS):
        value = part_ref[chip].astype(jnp.float32)
        total += value * value
        scaled[:, chip * 128 : (chip + 1) * 128] = (value * both_rows(gains, chip)).astype(jnp.bfloat16)
    stat = jnp.sum(total[:ROWS] + total[ROWS:], axis=1, keepdims=True) / D
    scale = lax.rsqrt(stat + 1e-05)
    rows = pl.ds(pl.multiple_of(core * (GU_ROWS // 2), GU_ROWS // 2), GU_ROWS // 2)

    def product(tile):
        acc = acc_ref[:, tile * 256 : (tile + 1) * 256] + jnp.dot(
            scaled[...], weight_ref[rows, tile * 256 : (tile + 1) * 256], preferred_element_type=jnp.float32
        )
        return fold(acc[:ROWS], acc[ROWS:], 0) * scale

    pieces = []
    for pair in range(3):
        gate = product(pair)
        up = product(pair + 3)
        pieces.append((gate / (1.0 + jnp.exp(-gate)) * up).astype(jnp.bfloat16))
    both = product(6)
    last = both / (1.0 + jnp.exp(-both)) * pltpu.roll(both, 64, 1)
    low = lax.broadcasted_iota(jnp.int32, (ROWS, 128), 1) < 64
    pieces.append(jnp.where(low, last, 0.0).astype(jnp.bfloat16))
    hidden = jnp.dot(
        jnp.concatenate(pieces, axis=1), order_ref[...], preferred_element_type=jnp.float32
    ).astype(jnp.bfloat16)
    hidden = jnp.concatenate([hidden[:, :256], hidden[:, 256:]], axis=0)
    for chip in range(CHIPS):
        out_ref[chip] = hidden


def mixed_of(part_ref, weight_ref):
    left = jnp.concatenate([part_ref[chip] for chip in range(CHIPS)], axis=1)
    acc = jnp.dot(left, weight_ref[: DN_ROWS // 2, :], preferred_element_type=jnp.float32)
    even, odd = acc[:ROWS], acc[ROWS:]
    return jnp.concatenate([fold(even, odd, 0), fold(even, odd, 256)], axis=1)


def send_kernel(part_ref, weight_ref, out_ref):
    out_ref[...] = mixed_of(part_ref, weight_ref)


def keep_kernel(part_ref, weight_ref, got_ref, taken_ref, order_ref, back_ref, out_ref, next_ref):
    taken = jnp.concatenate([taken_ref[:ROWS], taken_ref[ROWS:]], axis=1)
    taken = jnp.dot(taken, back_ref[...], preferred_element_type=jnp.float32)
    produced = (taken + (mixed_of(part_ref, weight_ref) + got_ref[...])).astype(jnp.bfloat16)
    out_ref[...] = produced
    ordered = jnp.dot(produced, order_ref[...], preferred_element_type=jnp.float32).astype(jnp.bfloat16)
    next_ref[...] = jnp.concatenate([ordered[:, :128], ordered[:, 128:]], axis=0)


def prepare_kernel(x_ref, norm_ref, order_ref, *refs):
    firsts, gain_ref, rows_ref = refs[:-2], refs[-2], refs[-1]
    for device in range(2 * CHIPS):
        rows_ref[device : device + 1, :] = norm_ref[:, device * 256 : (device + 1) * 256]
    left = rows_ref[...]
    gain = jnp.zeros(left.shape, jnp.float32)
    for _ in range(3):
        piece = left.astype(jnp.bfloat16)
        left = left - piece.astype(jnp.float32)
        gain = gain + jnp.dot(piece, order_ref[...], preferred_element_type=jnp.float32)
    for device in range(2 * CHIPS):
        at = 2 * (device % 2 * CHIPS + device // 2)
        for p in range(2):
            gain_ref[at + p : at + p + 1, :] = gain[device : device + 1, p * 128 : (p + 1) * 128]
    ordered = jnp.dot(x_ref[...], order_ref[...], preferred_element_type=jnp.float32).astype(jnp.bfloat16)
    for group, ref in enumerate(firsts):
        part = ordered[group * ROWS : (group + 1) * ROWS]
        ref[...] = jnp.concatenate([part[:, :128], part[:, 128:]], axis=0)


def pick_kernel(place_ref, *refs):
    made, out_ref = refs[:-1], refs[-1]
    groups = out_ref.shape[0] // ROWS
    for segment in range(len(made) - groups + 1):

        @pl.when(place_ref[0] == segment)
        def _():
            for group in range(groups):
                out_ref[group * ROWS : (group + 1) * ROWS, :] = made[group + segment][...]


VMEM = pl.BlockSpec(memory_space=pltpu.VMEM)
SMEM = pl.BlockSpec(memory_space=pltpu.SMEM)


def resident(weight):
    return pltpu.with_memory_space_constraint(weight, pltpu.VMEM)


def cost(products):
    return pl.CostEstimate(flops=2 * 128 * products, bytes_accessed=2 * MIB, transcendentals=0)


def prepare(x_in, norm_gain, x_order):
    groups = x_in.shape[0] // ROWS
    return pl.pallas_call(
        prepare_kernel,
        out_shape=[jax.ShapeDtypeStruct((2 * ROWS, 128), jnp.bfloat16)] * groups
        + [jax.ShapeDtypeStruct((4 * CHIPS, 128), jnp.float32)],
        in_specs=[VMEM] * 3,
        out_specs=[VMEM] * (groups + 1),
        scratch_shapes=[pltpu.VMEM((2 * CHIPS, 256), jnp.float32)],
        compiler_params=pltpu.CompilerParams(vmem_limit_bytes=8 * MIB),
        name="prepare",
    )(x_in, norm_gain, x_order)


def call_near(core, part, gain, weight):
    return pl.pallas_call(
        near_kernel,
        out_shape=(
            jax.ShapeDtypeStruct((2 * ROWS, GU_COLS), jnp.float32),
            jax.ShapeDtypeStruct((2 * ROWS, 128), jnp.float32),
        ),
        in_specs=[SMEM, VMEM, VMEM, VMEM],
        out_specs=(VMEM, VMEM),
        scratch_shapes=[pltpu.VMEM((2 * ROWS, GU_ROWS // 2), jnp.bfloat16)],
        compiler_params=pltpu.CompilerParams(vmem_limit_bytes=16 * MIB),
        cost_estimate=cost(GU_ROWS * GU_COLS // 2),
        name="near",
    )(core, part, gain, resident(weight))


def call_far(core, part, gain, weight, order, acc, square):
    return pl.pallas_call(
        far_kernel,
        out_shape=jax.ShapeDtypeStruct((CHIPS, 2 * ROWS, 256), jnp.bfloat16),
        in_specs=[SMEM] + [VMEM] * 6,
        out_specs=VMEM,
        scratch_shapes=[pltpu.VMEM((2 * ROWS, GU_ROWS // 2), jnp.bfloat16)],
        compiler_params=pltpu.CompilerParams(vmem_limit_bytes=16 * MIB),
        cost_estimate=cost(GU_ROWS * GU_COLS // 2),
        name="far",
    )(core, part, gain, resident(weight), order, acc, square)


def call_send(part, weight):
    return pl.pallas_call(
        send_kernel,
        out_shape=jax.ShapeDtypeStruct((ROWS, 256), jnp.float32),
        in_specs=[VMEM] * 2,
        out_specs=VMEM,
        compiler_params=pltpu.CompilerParams(vmem_limit_bytes=16 * MIB),
        cost_estimate=cost(DN_ROWS * DN_COLS // 2),
        name="send",
    )(part, resident(weight))


def call_keep(part, weight, got, taken, order, back):
    return pl.pallas_call(
        keep_kernel,
        out_shape=(
            jax.ShapeDtypeStruct((ROWS, 256), jnp.bfloat16),
            jax.ShapeDtypeStruct((2 * ROWS, 128), jnp.bfloat16),
        ),
        in_specs=[VMEM] * 6,
        out_specs=(VMEM, VMEM),
        compiler_params=pltpu.CompilerParams(vmem_limit_bytes=16 * MIB),
        cost_estimate=cost(DN_ROWS * DN_COLS // 2),
        name="keep",
    )(part, resident(weight), got, taken, order, back)


def call_pick(place, made, groups):
    return pl.pallas_call(
        pick_kernel,
        out_shape=jax.ShapeDtypeStruct((groups * ROWS, 256), jnp.bfloat16),
        in_specs=[SMEM] + [VMEM] * len(made),
        out_specs=VMEM,
        compiler_params=pltpu.CompilerParams(vmem_limit_bytes=4 * MIB),
        name="pick",
    )(place, *made)


def orders():
    source = jnp.arange(256)
    goal = (source % 2) * 128 + source // 64 * 32 + source % 64 // 2
    x_order = (goal[:, None] == jnp.arange(256)[None, :]).astype(jnp.bfloat16)
    source = jnp.arange(512)
    goal = (source % 2) * 256 + source // 64 * 32 + source % 64 // 2
    h_order = (goal[:, None] == jnp.arange(512)[None, :]).astype(jnp.bfloat16)
    return x_order, h_order


def exchanged(value):
    same_core = [[2 * chip + core for chip in range(CHIPS)] for core in range(2)]
    return lax.all_to_all(value, "tensor", 0, 0, axis_index_groups=same_core)


def swapped(value):
    return lax.ppermute(value, "tensor", [(i, i ^ 1) for i in range(2 * CHIPS)])


def local(x_in, norm_gain, in_index, gate_blocks, up_blocks, out_index, down_blocks):
    segment_count = lax.axis_size("segment")
    segment_at = lax.axis_index("segment")
    core = (lax.axis_index("tensor") % 2).astype(jnp.int32)[None]
    tokens = x_in.shape[0]
    group_count = tokens // ROWS
    tick_count = group_count + segment_count - 1
    x_order, h_order = orders()
    x_back = x_order.T
    *firsts, gain = prepare(x_in, norm_gain, x_order)
    is_first = jnp.broadcast_to(segment_at == 0, (8, 128)).astype(jnp.bfloat16)
    place = segment_at.astype(jnp.int32)[None]
    to_wide, to_down = in_goals(in_index[0]), out_goals(out_index[0], core[0])
    to_wide, to_down, core, place, x_order, x_back, h_order, gain, firsts, is_first = lax.optimization_barrier(
        (to_wide, to_down, core, place, x_order, x_back, h_order, gain, firsts, is_first)
    )
    carried = None
    made = []
    hops = [(i, i + 1) for i in range(segment_count - 1)]
    for tick in range(tick_count):
        taken = firsts[min(tick, group_count - 1)]
        if carried is not None:
            taken = jnp.where(jnp.tile(is_first, (2 * ROWS // 8, 1)) > 0, taken, carried)
        mine = exchanged(jnp.broadcast_to(taken[None], (CHIPS, 2 * ROWS, 128)))
        if tick == 0:
            mine, to_wide, to_down = lax.optimization_barrier((mine, to_wide, to_down))
            wide = densify_wide(to_wide, gate_blocks[0], up_blocks[0])
            down, lent = densify_down(to_down, down_blocks[0])
            borrowed = swapped(lent)
        other = swapped(mine)
        acc, square = call_near(core, mine, gain, wide)
        hidden = call_far(core, other, gain, wide, h_order, acc, square)
        mine = exchanged(hidden)
        got = swapped(call_send(mine, borrowed))
        produced, ordered = call_keep(mine, down, got, taken, x_order, x_back)
        made.append(produced)
        if tick + 1 < tick_count:
            carried = lax.ppermute(ordered, "segment", hops)
    return call_pick(place, made, group_count)[None]


def solution(mesh):
    placed = (
        P("replica", "tensor"),
        P("segment", None),
        P("segment", "tensor", None),
        P("segment", "tensor", None, None),
        P("segment", "tensor", None, None),
        P("segment", "tensor", None),
        P("segment", "tensor", None, None),
    )
    return jax.shard_map(
        local,
        mesh=mesh,
        in_specs=placed,
        out_specs=P("segment", "replica", "tensor"),
        check_vma=False,
    )
```

```python
import functools

import jax
import jax.numpy as jnp
from jax import lax
from jax.experimental import pallas as pl
from jax.experimental.pallas import tpu as pltpu
from jax.sharding import PartitionSpec as P

D = 8192
FFW = 14336
BS = 64
CHIPS = 16
ROWS = 64
GU_ROWS = D // 2
GU_COLS = 14 * 128
DN_ROWS = 32 * 256
DN_COLS = 4 * 128
MIB = 1 << 20


def clear(target):
    rows, cols = target.shape

    def one(at, _):
        target[pl.ds(pl.multiple_of(at * 32, 32), 32), :] = jnp.zeros((32, cols), target.dtype)
        return 0

    lax.fori_loop(0, rows // 32, one, 0)


def wide_pack_kernel(goal_ref, gate_hbm, up_hbm, target, buf, spread, sems):
    tiles, slots = goal_ref.shape
    for which, source in enumerate((gate_hbm, up_hbm)):
        for tile in range(tiles):
            at = which * tiles + tile
            pltpu.make_async_copy(source.at[tile], buf.at[at], sems.at[at]).start()
    clear(target)

    def place(chunk, count, first, half, tile, column):
        for group in range(0, count, 8):
            for part in range(32):
                spread[half, group * 32 + part * 8 : group * 32 + part * 8 + 8, :] = chunk[
                    group : group + 8, part * 128 : (part + 1) * 128
                ]
        for row in range(count):
            goal = pl.multiple_of(goal_ref[tile, first + row], 32)
            piece = spread[half, pl.ds(row // 8 * 256 + row % 8, 32, stride=8), :]
            target[pl.ds(goal, 32), pl.ds(column, 128)] = piece.astype(target.dtype)

    def one(at, _):
        pltpu.make_async_copy(gate_hbm.at[0], buf.at[at], sems.at[at]).wait()
        which = (at >= tiles).astype(jnp.int32)
        tile = at - which * tiles
        last = tiles - 1
        column = pl.multiple_of(jnp.where(tile == last, 2 * last + which, which * last + tile) * 128, 128)

        def pair(step, _):
            for half in range(2):
                first = pl.multiple_of(step * 32 + half * 16, 16)
                chunk = buf[at, pl.ds(first, 16), :].astype(jnp.float32)
                place(chunk, 16, first, half, tile, column)
            return 0

        lax.fori_loop(0, slots // 32, pair, 0)
        done = slots // 32 * 32
        half = 0
        while done < slots:
            count = min(16, slots - done)
            chunk = buf[at, done : done + count, :].astype(jnp.float32)
            place(chunk, count, done, half, tile, column)
            done += count
            half = 1 - half
        return 0

    lax.fori_loop(0, 2 * tiles, one, 0)


def down_pack_kernel(goal_ref, source, near, far, buf, spread, sems):
    tiles, slots = goal_ref.shape[0] // 2, goal_ref.shape[1]
    parts = 7
    size = slots // parts
    for part in range(parts):
        pltpu.make_async_copy(
            source.at[pl.ds(part * size, size)], buf.at[pl.ds(part * size, size)], sems.at[part]
        ).start()
    clear(near)
    clear(far)

    def one(part, _):
        pltpu.make_async_copy(
            source.at[pl.ds(0, size)], buf.at[pl.ds(part * size, size)], sems.at[part]
        ).wait()

        def step(at, _):
            for half in range(3):
                slot = part * size + at * 6 + half * 2
                for inner in range(2):
                    chunk = buf[slot + inner].astype(jnp.float32)
                    for lane in range(32):
                        spread[half, lane * 8 + inner * 4 : lane * 8 + inner * 4 + 4, :] = chunk[
                            :, lane * 128 : (lane + 1) * 128
                        ]
                for inner in range(2):
                    for tile in range(tiles):
                        piece = spread[half, pl.ds(inner * 4 + tile, 32, stride=8), :].astype(near.dtype)
                        for which, target in enumerate((near, far)):
                            goal = pl.multiple_of(goal_ref[which * tiles + tile, slot + inner], 32)
                            target[pl.ds(goal, 32), tile * 128 : (tile + 1) * 128] = piece
            return 0

        lax.fori_loop(0, size // 6, step, 0)
        return 0

    lax.fori_loop(0, parts, one, 0)


def pack(kernel, goals, sources, buf, spread, copies, shape, results, name):
    sources = [pltpu.with_memory_space_constraint(source, pltpu.HBM) for source in sources]
    return pl.pallas_call(
        kernel,
        out_shape=[pltpu.VMEM(shape, jnp.bfloat16)] * results,
        in_specs=[pl.BlockSpec(memory_space=pltpu.SMEM)]
        + [pl.BlockSpec(memory_space=pltpu.HBM)] * len(sources),
        out_specs=[pl.BlockSpec(memory_space=pltpu.VMEM)] * results,
        scratch_shapes=[
            pltpu.VMEM(buf, jnp.bfloat16),
            pltpu.VMEM(spread + (128,), jnp.float32),
            pltpu.SemaphoreType.DMA((copies,)),
        ],
        compiler_params=pltpu.CompilerParams(vmem_limit_bytes=12 * MIB),
        cost_estimate=pl.CostEstimate(flops=0, bytes_accessed=40 * MIB, transcendentals=0),
        name=name,
    )(goals, *sources)


def densify_wide(goals, gate_blocks, up_blocks):
    tiles, slots = goals.shape
    buf = (2 * tiles, slots, BS * BS)
    shape = (GU_ROWS + 32, GU_COLS)
    sources = (gate_blocks, up_blocks)
    return pack(wide_pack_kernel, goals, sources, buf, (2, 512), 2 * tiles, shape, 1, "pack_wide")[0]


def densify_down(goals, blocks):
    tiles, slots = blocks.shape[:2]
    shape = (DN_ROWS // 2 + 32, DN_COLS)
    blocks = jnp.transpose(blocks, (1, 0, 2))
    buf = (slots, tiles, BS * BS)
    return pack(down_pack_kernel, goals, (blocks,), buf, (3, 256), 7, shape, 2, "pack_down")


def in_goals(index):
    row = (((index >> 2) & 1) * CHIPS + (index >> 3)) * 128 + (index & 3) * 32
    return jnp.where(index >= 0, row, GU_ROWS)


def out_goals(index, core):
    device = lax.div(index, jnp.int32(7))
    row = (device >> 1) * 256 + (index - device * 7) * 32
    near = (device & 1) == core
    trash = DN_ROWS // 2
    return jnp.concatenate(
        [
            jnp.where((index >= 0) & near, row, trash),
            jnp.where((index >= 0) & jnp.logical_not(near), row, trash),
        ],
        axis=0,
    )


def fold(even, odd, at):
    low = lax.broadcasted_iota(jnp.int32, (ROWS, 128), 1) < 64
    e0, e1 = even[:, at : at + 128], even[:, at + 128 : at + 256]
    o0, o1 = odd[:, at : at + 128], odd[:, at + 128 : at + 256]
    return jnp.where(low, e0, o1) + pltpu.roll(jnp.where(low, e1, o0), 64, 1)


def near_kernel(core_ref, part_ref, gain_ref, weight_ref, acc_ref, square_ref, scaled):
    core = core_ref[0]
    total = jnp.zeros((2 * ROWS, 128), jnp.float32)
    gains = gain_ref[pl.ds(pl.multiple_of(core * 32, 32), 32), :]
    for chip in range(CHIPS):
        value = part_ref[chip].astype(jnp.float32)
        total += value * value
        scaled[:, chip * 128 : (chip + 1) * 128] = (value * both_rows(gains, chip)).astype(jnp.bfloat16)
    square_ref[...] = total
    rows = pl.ds(pl.multiple_of(core * (GU_ROWS // 2), GU_ROWS // 2), GU_ROWS // 2)
    for tile in range(7):
        acc_ref[:, tile * 256 : (tile + 1) * 256] = jnp.dot(
            scaled[...], weight_ref[rows, tile * 256 : (tile + 1) * 256], preferred_element_type=jnp.float32
        )


def both_rows(gains, chip):
    return jnp.concatenate(
        [jnp.broadcast_to(gains[2 * chip + p : 2 * chip + p + 1], (ROWS, 128)) for p in range(2)], axis=0
    )


def far_kernel(core_ref, part_ref, gain_ref, weight_ref, order_ref, acc_ref, square_ref, out_ref, scaled):
    core = 1 - core_ref[0]
    total = square_ref[...]
    gains = gain_ref[pl.ds(pl.multiple_of(core * 32, 32), 32), :]
    for chip in range(CHIPS):
        value = part_ref[chip].astype(jnp.float32)
        total += value * value
        scaled[:, chip * 128 : (chip + 1) * 128] = (value * both_rows(gains, chip)).astype(jnp.bfloat16)
    stat = jnp.sum(total[:ROWS] + total[ROWS:], axis=1, keepdims=True) / D
    scale = lax.rsqrt(stat + 1e-05)
    rows = pl.ds(pl.multiple_of(core * (GU_ROWS // 2), GU_ROWS // 2), GU_ROWS // 2)

    def product(tile):
        acc = acc_ref[:, tile * 256 : (tile + 1) * 256] + jnp.dot(
            scaled[...], weight_ref[rows, tile * 256 : (tile + 1) * 256], preferred_element_type=jnp.float32
        )
        return fold(acc[:ROWS], acc[ROWS:], 0) * scale

    pieces = []
    for pair in range(3):
        gate = product(pair)
        up = product(pair + 3)
        pieces.append((gate / (1.0 + jnp.exp(-gate)) * up).astype(jnp.bfloat16))
    both = product(6)
    last = both / (1.0 + jnp.exp(-both)) * pltpu.roll(both, 64, 1)
    low = lax.broadcasted_iota(jnp.int32, (ROWS, 128), 1) < 64
    pieces.append(jnp.where(low, last, 0.0).astype(jnp.bfloat16))
    hidden = jnp.dot(
        jnp.concatenate(pieces, axis=1), order_ref[...], preferred_element_type=jnp.float32
    ).astype(jnp.bfloat16)
    hidden = jnp.concatenate([hidden[:, :256], hidden[:, 256:]], axis=0)
    for chip in range(CHIPS):
        out_ref[chip] = hidden


def mixed_of(part_ref, weight_ref):
    left = jnp.concatenate([part_ref[chip] for chip in range(CHIPS)], axis=1)
    acc = jnp.dot(left, weight_ref[: DN_ROWS // 2, :], preferred_element_type=jnp.float32)
    even, odd = acc[:ROWS], acc[ROWS:]
    return jnp.concatenate([fold(even, odd, 0), fold(even, odd, 256)], axis=1)


def send_kernel(part_ref, weight_ref, out_ref):
    out_ref[...] = mixed_of(part_ref, weight_ref)


def keep_kernel(part_ref, weight_ref, got_ref, taken_ref, order_ref, back_ref, out_ref, next_ref):
    taken = jnp.concatenate([taken_ref[:ROWS], taken_ref[ROWS:]], axis=1)
    taken = jnp.dot(taken, back_ref[...], preferred_element_type=jnp.float32)
    produced = (taken + (mixed_of(part_ref, weight_ref) + got_ref[...])).astype(jnp.bfloat16)
    out_ref[...] = produced
    ordered = jnp.dot(produced, order_ref[...], preferred_element_type=jnp.float32).astype(jnp.bfloat16)
    next_ref[...] = jnp.concatenate([ordered[:, :128], ordered[:, 128:]], axis=0)


def gain_kernel(norm_ref, order_ref, gain_ref, rows_ref):
    for device in range(2 * CHIPS):
        rows_ref[device : device + 1, :] = norm_ref[:, device * 256 : (device + 1) * 256]
    left = rows_ref[...]
    gain = jnp.zeros(left.shape, jnp.float32)
    for _ in range(3):
        piece = left.astype(jnp.bfloat16)
        left = left - piece.astype(jnp.float32)
        gain = gain + jnp.dot(piece, order_ref[...], preferred_element_type=jnp.float32)
    for device in range(2 * CHIPS):
        at = 2 * (device % 2 * CHIPS + device // 2)
        for p in range(2):
            gain_ref[at + p : at + p + 1, :] = gain[device : device + 1, p * 128 : (p + 1) * 128]


def prepare_kernel(x_ref, order_ref, *firsts):
    ordered = jnp.dot(x_ref[...], order_ref[...], preferred_element_type=jnp.float32).astype(jnp.bfloat16)
    for group, ref in enumerate(firsts):
        part = ordered[group * ROWS : (group + 1) * ROWS]
        ref[...] = jnp.concatenate([part[:, :128], part[:, 128:]], axis=0)


def line_kernel(at_ref, *refs):
    for shift, ref in enumerate(refs[:4]):
        refs[-1][(at_ref[0] - shift) & 3] = ref[...]


def plane_kernel(at_ref, *refs):
    for shift, ref in enumerate(refs[:4]):
        for line in range(4):
            refs[-1][line * 4 + ((at_ref[0] - shift) & 3)] = ref[line]


def pick_kernel(place_ref, *refs):
    made, out_ref = refs[:-1], refs[-1]
    groups = out_ref.shape[0] // ROWS
    for segment in range(len(made) - groups + 1):

        @pl.when(place_ref[0] == segment)
        def _():
            for group in range(groups):
                out_ref[group * ROWS : (group + 1) * ROWS, :] = made[group + segment][...]


VMEM = pl.BlockSpec(memory_space=pltpu.VMEM)
SMEM = pl.BlockSpec(memory_space=pltpu.SMEM)


def resident(weight):
    return pltpu.with_memory_space_constraint(weight, pltpu.VMEM)


def cost(products):
    return pl.CostEstimate(flops=2 * 128 * products, bytes_accessed=2 * MIB, transcendentals=0)


def prepare(x_in, x_order):
    groups = x_in.shape[0] // ROWS
    return pl.pallas_call(
        prepare_kernel,
        out_shape=[jax.ShapeDtypeStruct((2 * ROWS, 128), jnp.bfloat16)] * groups,
        in_specs=[VMEM] * 2,
        out_specs=[VMEM] * groups,
        compiler_params=pltpu.CompilerParams(vmem_limit_bytes=4 * MIB),
        name="prepare",
    )(x_in, x_order)


def gains_of(norm_gain, x_order):
    return pl.pallas_call(
        gain_kernel,
        out_shape=jax.ShapeDtypeStruct((4 * CHIPS, 128), jnp.float32),
        in_specs=[VMEM] * 2,
        out_specs=VMEM,
        scratch_shapes=[pltpu.VMEM((2 * CHIPS, 256), jnp.float32)],
        compiler_params=pltpu.CompilerParams(vmem_limit_bytes=4 * MIB),
        name="gains",
    )(norm_gain, x_order)


def placed_by(kernel, at, parts, count):
    return pl.pallas_call(
        kernel,
        out_shape=jax.ShapeDtypeStruct((count,) + parts[0].shape[-2:], parts[0].dtype),
        in_specs=[SMEM] + [VMEM] * len(parts),
        out_specs=VMEM,
        compiler_params=pltpu.CompilerParams(vmem_limit_bytes=8 * MIB),
        name="placed",
    )(at, *parts)


def shifted_all(value, along_x):
    parts = [value]
    for shift in range(1, 4):
        pairs = []
        for x in range(4):
            for y in range(4):
                goal = ((x + shift) % 4 * 4 + y) if along_x else (x * 4 + (y + shift) % 4)
                pairs += [(2 * (x * 4 + y) + core, 2 * goal + core) for core in range(2)]
        parts.append(lax.ppermute(value, "tensor", pairs))
    return parts


def call_near(core, part, gain, weight):
    return pl.pallas_call(
        near_kernel,
        out_shape=(
            jax.ShapeDtypeStruct((2 * ROWS, GU_COLS), jnp.float32),
            jax.ShapeDtypeStruct((2 * ROWS, 128), jnp.float32),
        ),
        in_specs=[SMEM, VMEM, VMEM, VMEM],
        out_specs=(VMEM, VMEM),
        scratch_shapes=[pltpu.VMEM((2 * ROWS, GU_ROWS // 2), jnp.bfloat16)],
        compiler_params=pltpu.CompilerParams(vmem_limit_bytes=16 * MIB),
        cost_estimate=cost(GU_ROWS * GU_COLS // 2),
        name="near",
    )(core, part, gain, resident(weight))


def call_far(core, part, gain, weight, order, acc, square):
    return pl.pallas_call(
        far_kernel,
        out_shape=jax.ShapeDtypeStruct((CHIPS, 2 * ROWS, 256), jnp.bfloat16),
        in_specs=[SMEM] + [VMEM] * 6,
        out_specs=VMEM,
        scratch_shapes=[pltpu.VMEM((2 * ROWS, GU_ROWS // 2), jnp.bfloat16)],
        compiler_params=pltpu.CompilerParams(vmem_limit_bytes=16 * MIB),
        cost_estimate=cost(GU_ROWS * GU_COLS // 2),
        name="far",
    )(core, part, gain, resident(weight), order, acc, square)


def call_send(part, weight):
    return pl.pallas_call(
        send_kernel,
        out_shape=jax.ShapeDtypeStruct((ROWS, 256), jnp.float32),
        in_specs=[VMEM] * 2,
        out_specs=VMEM,
        compiler_params=pltpu.CompilerParams(vmem_limit_bytes=16 * MIB),
        cost_estimate=cost(DN_ROWS * DN_COLS // 2),
        name="send",
    )(part, resident(weight))


def call_keep(part, weight, got, taken, order, back):
    return pl.pallas_call(
        keep_kernel,
        out_shape=(
            jax.ShapeDtypeStruct((ROWS, 256), jnp.bfloat16),
            jax.ShapeDtypeStruct((2 * ROWS, 128), jnp.bfloat16),
        ),
        in_specs=[VMEM] * 6,
        out_specs=(VMEM, VMEM),
        compiler_params=pltpu.CompilerParams(vmem_limit_bytes=16 * MIB),
        cost_estimate=cost(DN_ROWS * DN_COLS // 2),
        name="keep",
    )(part, resident(weight), got, taken, order, back)


def call_pick(place, made, groups):
    return pl.pallas_call(
        pick_kernel,
        out_shape=jax.ShapeDtypeStruct((groups * ROWS, 256), jnp.bfloat16),
        in_specs=[SMEM] + [VMEM] * len(made),
        out_specs=VMEM,
        compiler_params=pltpu.CompilerParams(vmem_limit_bytes=4 * MIB),
        name="pick",
    )(place, *made)


def orders():
    source = jnp.arange(256)
    goal = (source % 2) * 128 + source // 64 * 32 + source % 64 // 2
    x_order = (goal[:, None] == jnp.arange(256)[None, :]).astype(jnp.bfloat16)
    source = jnp.arange(512)
    goal = (source % 2) * 256 + source // 64 * 32 + source % 64 // 2
    h_order = (goal[:, None] == jnp.arange(512)[None, :]).astype(jnp.bfloat16)
    return x_order, h_order


def exchanged(value):
    same_core = [[2 * chip + core for chip in range(CHIPS)] for core in range(2)]
    return lax.all_to_all(value, "tensor", 0, 0, axis_index_groups=same_core)


def swapped(value):
    return lax.ppermute(value, "tensor", [(i, i ^ 1) for i in range(2 * CHIPS)])


def local(x_in, norm_gain, in_index, gate_blocks, up_blocks, out_index, down_blocks):
    segment_count = lax.axis_size("segment")
    segment_at = lax.axis_index("segment")
    tensor_at = lax.axis_index("tensor").astype(jnp.int32)
    core = (tensor_at & 1)[None]
    tokens = x_in.shape[0]
    group_count = tokens // ROWS
    tick_count = group_count + segment_count - 1
    x_order, h_order = orders()
    x_back = x_order.T
    firsts = prepare(x_in, x_order)
    is_first = jnp.broadcast_to(segment_at == 0, (8, 128)).astype(jnp.bfloat16)
    place = segment_at.astype(jnp.int32)[None]
    x_at, y_at = (tensor_at >> 3)[None], ((tensor_at >> 1) & 3)[None]
    core, place, x_at, y_at, x_order, x_back, h_order, firsts, is_first = lax.optimization_barrier(
        (core, place, x_at, y_at, x_order, x_back, h_order, firsts, is_first)
    )

    carried = None
    made = []
    hops = [(i, i + 1) for i in range(segment_count - 1)]
    for tick in range(tick_count):
        taken = firsts[min(tick, group_count - 1)]
        if carried is not None:
            taken = jnp.where(jnp.tile(is_first, (2 * ROWS // 8, 1)) > 0, taken, carried)
        if tick == 0:
            parts = shifted_all(taken, True)
            out_now, norm_gain, core = lax.optimization_barrier((out_index[0], norm_gain, core))
            gain = gains_of(norm_gain, x_order)
            down, lent = densify_down(out_goals(out_now, core[0]), down_blocks[0])
            line = placed_by(line_kernel, x_at, parts + [resident(down)], 4)
            in_now, line = lax.optimization_barrier((in_index[0], line))
            parts = shifted_all(line, False)
            wide = densify_wide(in_goals(in_now), gate_blocks[0], up_blocks[0])
            mine = placed_by(plane_kernel, y_at, parts + [resident(wide)], CHIPS)
        else:
            mine = exchanged(jnp.broadcast_to(taken[None], (CHIPS, 2 * ROWS, 128)))
        other = swapped(mine)
        acc, square = call_near(core, mine, gain, wide)
        hidden = call_far(core, other, gain, wide, h_order, acc, square)
        if tick == 0:
            hidden, lent = lax.optimization_barrier((hidden, lent))
            borrowed = swapped(lent)
        mine = exchanged(hidden)
        got = swapped(call_send(mine, borrowed))
        produced, ordered = call_keep(mine, down, got, taken, x_order, x_back)
        made.append(produced)
        if tick + 1 < tick_count:
            carried = lax.ppermute(ordered, "segment", hops)
    return call_pick(place, made, group_count)[None]


def solution(mesh):
    placed = (
        P("replica", "tensor"),
        P("segment", None),
        P("segment", "tensor", None),
        P("segment", "tensor", None, None),
        P("segment", "tensor", None, None),
        P("segment", "tensor", None),
        P("segment", "tensor", None, None),
    )
    return jax.shard_map(
        local,
        mesh=mesh,
        in_specs=placed,
        out_specs=P("segment", "replica", "tensor"),
        check_vma=False,
    )
```

```python
import functools

import jax
import jax.numpy as jnp
from jax import lax
from jax.experimental import pallas as pl
from jax.experimental.pallas import tpu as pltpu
from jax.sharding import PartitionSpec as P

D = 8192
FFW = 14336
BS = 64
CHIPS = 16
ROWS = 64
KEPT = 112
GU_ROWS = D // 2
GU_COLS = 14 * 128
DN_ROWS = 32 * 256
DN_COLS = 4 * 128
MIB = 1 << 20


def clear(target):
    rows, cols = target.shape

    def one(at, _):
        target[pl.ds(pl.multiple_of(at * 32, 32), 32), :] = jnp.zeros((32, cols), target.dtype)
        return 0

    lax.fori_loop(0, rows // 32, one, 0)


def wide_pack_kernel(goal_ref, gate_hbm, up_hbm, target, buf, spread, sems):
    tiles, slots = goal_ref.shape
    for which, source in enumerate((gate_hbm, up_hbm)):
        for tile in range(tiles):
            at = which * tiles + tile
            pltpu.make_async_copy(source.at[tile], buf.at[at], sems.at[at]).start()
    clear(target)

    def place(chunk, count, first, half, tile, column):
        for group in range(0, count, 8):
            for part in range(32):
                spread[half, group * 32 + part * 8 : group * 32 + part * 8 + 8, :] = chunk[
                    group : group + 8, part * 128 : (part + 1) * 128
                ]
        for row in range(count):
            goal = pl.multiple_of(goal_ref[tile, first + row], 32)
            piece = spread[half, pl.ds(row // 8 * 256 + row % 8, 32, stride=8), :]
            target[pl.ds(goal, 32), pl.ds(column, 128)] = piece.astype(target.dtype)

    def one(at, _):
        pltpu.make_async_copy(gate_hbm.at[0], buf.at[at], sems.at[at]).wait()
        which = (at >= tiles).astype(jnp.int32)
        tile = at - which * tiles
        last = tiles - 1
        column = pl.multiple_of(jnp.where(tile == last, 2 * last + which, which * last + tile) * 128, 128)

        def pair(step, _):
            for half in range(2):
                first = pl.multiple_of(step * 32 + half * 16, 16)
                chunk = buf[at, pl.ds(first, 16), :].astype(jnp.float32)
                place(chunk, 16, first, half, tile, column)
            return 0

        lax.fori_loop(0, slots // 32, pair, 0)
        done = slots // 32 * 32
        half = 0
        while done < slots:
            count = min(16, slots - done)
            chunk = buf[at, done : done + count, :].astype(jnp.float32)
            place(chunk, count, done, half, tile, column)
            done += count
            half = 1 - half
        return 0

    lax.fori_loop(0, 2 * tiles, one, 0)


def down_pack_kernel(near_goal, far_goal, source, near, far, buf, spread, sems):
    tiles, slots = near_goal.shape
    parts = 7
    size = slots // parts
    for part in range(parts):
        pltpu.make_async_copy(
            source.at[pl.ds(part * size, size)], buf.at[pl.ds(part * size, size)], sems.at[part]
        ).start()
    clear(near)
    clear(far)

    def one(part, _):
        pltpu.make_async_copy(
            source.at[pl.ds(0, size)], buf.at[pl.ds(part * size, size)], sems.at[part]
        ).wait()

        def step(at, _):
            for half in range(3):
                slot = part * size + at * 6 + half * 2
                for inner in range(2):
                    chunk = buf[slot + inner].astype(jnp.float32)
                    for lane in range(32):
                        spread[half, lane * 8 + inner * 4 : lane * 8 + inner * 4 + 4, :] = chunk[
                            :, lane * 128 : (lane + 1) * 128
                        ]
                for inner in range(2):
                    for tile in range(tiles):
                        piece = spread[half, pl.ds(inner * 4 + tile, 32, stride=8), :].astype(near.dtype)
                        for goal_ref, target in ((near_goal, near), (far_goal, far)):
                            goal = pl.multiple_of(goal_ref[tile, slot + inner], 32)
                            target[pl.ds(goal, 32), tile * 128 : (tile + 1) * 128] = piece
            return 0

        lax.fori_loop(0, size // 6, step, 0)
        return 0

    lax.fori_loop(0, parts, one, 0)


def pack(kernel, goals, sources, buf, spread, copies, shape, results, name):
    sources = [pltpu.with_memory_space_constraint(source, pltpu.HBM) for source in sources]
    return pl.pallas_call(
        kernel,
        out_shape=[pltpu.VMEM(shape, jnp.bfloat16)] * results,
        in_specs=[pl.BlockSpec(memory_space=pltpu.SMEM)] * len(goals)
        + [pl.BlockSpec(memory_space=pltpu.HBM)] * len(sources),
        out_specs=[pl.BlockSpec(memory_space=pltpu.VMEM)] * results,
        scratch_shapes=[
            pltpu.VMEM(buf, jnp.bfloat16),
            pltpu.VMEM(spread + (128,), jnp.float32),
            pltpu.SemaphoreType.DMA((copies,)),
        ],
        compiler_params=pltpu.CompilerParams(vmem_limit_bytes=12 * MIB),
        cost_estimate=pl.CostEstimate(flops=0, bytes_accessed=40 * MIB, transcendentals=0),
        name=name,
    )(*goals, *sources)


def densify_wide(goals, gate_blocks, up_blocks):
    tiles, slots = goals.shape
    buf = (2 * tiles, slots, BS * BS)
    shape = (GU_ROWS + 32, GU_COLS)
    sources = (gate_blocks, up_blocks)
    return pack(wide_pack_kernel, (goals,), sources, buf, (2, 512), 2 * tiles, shape, 1, "pack_wide")[0]


def densify_down(goals, blocks):
    tiles, slots = blocks.shape[:2]
    shape = (DN_ROWS // 2 + 32, DN_COLS)
    blocks = jnp.transpose(blocks, (1, 0, 2))
    buf = (slots, tiles, BS * BS)
    return pack(down_pack_kernel, goals, (blocks,), buf, (3, 256), 7, shape, 2, "pack_down")


def in_goals(index):
    row = (((index >> 2) & 1) * CHIPS + (index >> 3)) * 128 + (index & 3) * 32
    return jnp.where(index >= 0, row, GU_ROWS)


def out_goals(index, core):
    device = lax.div(index, jnp.int32(7))
    row = (device >> 1) * 256 + (index - device * 7) * 32
    near = (device & 1) == core
    trash = DN_ROWS // 2
    kept = index >= 0
    return jnp.where(kept & near, row, trash), jnp.where(kept & jnp.logical_not(near), row, trash)


def fold(even, odd, at):
    low = lax.broadcasted_iota(jnp.int32, (ROWS, 128), 1) < 64
    e0, e1 = even[:, at : at + 128], even[:, at + 128 : at + 256]
    o0, o1 = odd[:, at : at + 128], odd[:, at + 128 : at + 256]
    return jnp.where(low, e0, o1) + pltpu.roll(jnp.where(low, e1, o0), 64, 1)


def near_kernel(core_ref, part_ref, gain_ref, weight_ref, acc_ref, square_ref, scaled):
    core = core_ref[0]
    total = jnp.zeros((2 * ROWS, 128), jnp.float32)
    gains = gain_ref[pl.ds(pl.multiple_of(core * 32, 32), 32), :]
    for chip in range(CHIPS):
        value = part_ref[chip].astype(jnp.float32)
        total += value * value
        scaled[:, chip * 128 : (chip + 1) * 128] = (value * both_rows(gains, chip)).astype(jnp.bfloat16)
    square_ref[...] = total
    rows = pl.ds(pl.multiple_of(core * (GU_ROWS // 2), GU_ROWS // 2), GU_ROWS // 2)
    for tile in range(7):
        acc_ref[:, tile * 256 : (tile + 1) * 256] = jnp.dot(
            scaled[...], weight_ref[rows, tile * 256 : (tile + 1) * 256], preferred_element_type=jnp.float32
        )


def both_rows(gains, chip):
    return jnp.concatenate(
        [jnp.broadcast_to(gains[2 * chip + p : 2 * chip + p + 1], (ROWS, 128)) for p in range(2)], axis=0
    )


def far_kernel(core_ref, part_ref, gain_ref, weight_ref, order_ref, acc_ref, square_ref, out_ref, scaled):
    core = 1 - core_ref[0]
    total = square_ref[...]
    gains = gain_ref[pl.ds(pl.multiple_of(core * 32, 32), 32), :]
    for chip in range(CHIPS):
        value = part_ref[chip].astype(jnp.float32)
        total += value * value
        scaled[:, chip * 128 : (chip + 1) * 128] = (value * both_rows(gains, chip)).astype(jnp.bfloat16)
    stat = jnp.sum(total[:ROWS] + total[ROWS:], axis=1, keepdims=True) / D
    scale = lax.rsqrt(stat + 1e-05)
    rows = pl.ds(pl.multiple_of(core * (GU_ROWS // 2), GU_ROWS // 2), GU_ROWS // 2)

    def product(tile):
        acc = acc_ref[:, tile * 256 : (tile + 1) * 256] + jnp.dot(
            scaled[...], weight_ref[rows, tile * 256 : (tile + 1) * 256], preferred_element_type=jnp.float32
        )
        return fold(acc[:ROWS], acc[ROWS:], 0) * scale

    pieces = []
    for pair in range(3):
        gate = product(pair)
        up = product(pair + 3)
        pieces.append((gate / (1.0 + jnp.exp(-gate)) * up).astype(jnp.bfloat16))
    both = product(6)
    last = both / (1.0 + jnp.exp(-both)) * pltpu.roll(both, 64, 1)
    low = lax.broadcasted_iota(jnp.int32, (ROWS, 128), 1) < 64
    pieces.append(jnp.where(low, last, 0.0).astype(jnp.bfloat16))
    hidden = jnp.dot(
        jnp.concatenate(pieces, axis=1), order_ref[...], preferred_element_type=jnp.float32
    )
    hidden = jnp.concatenate([hidden[:, :256], hidden[:, 256:]], axis=0)
    extra = []
    for slot in range(7):
        half = slot // 4 * 128
        piece = hidden[KEPT:, half : half + 128]
        extra.append(pltpu.roll(piece, (96 - slot % 4 * 32) % 128, 1) if slot % 4 != 3 else piece)
    spare = lax.broadcasted_iota(jnp.int32, (KEPT, 128), 1) >= 96
    right = jnp.where(spare, jnp.concatenate(extra, axis=0), hidden[:KEPT, 128:])
    hidden = jnp.concatenate([hidden[:KEPT, :128], right], axis=1).astype(jnp.bfloat16)
    for chip in range(CHIPS):
        out_ref[chip] = hidden


def mixed_of(part_ref, weight_ref):
    lane = lax.broadcasted_iota(jnp.int32, (16, 128), 1)
    pieces = []
    for chip in range(CHIPS):
        tails = []
        for half in range(2):
            tail = jnp.zeros((16, 128), jnp.float32)
            for slot in range(half * 4, min(half * 4 + 4, 7)):
                piece = part_ref[chip, slot * 16 : slot * 16 + 16, 128:].astype(jnp.float32)
                at = slot % 4 * 32
                piece = pltpu.roll(piece, (at + 32) % 128, 1) if at != 96 else piece
                tail = jnp.where((lane >= at) & (lane < at + 32), piece, tail)
            tails.append(tail)
        tail = jnp.concatenate(tails, axis=1).astype(jnp.bfloat16)
        pieces.append(jnp.concatenate([part_ref[chip], tail], axis=0))
    left = jnp.concatenate(pieces, axis=1)
    acc = jnp.dot(left, weight_ref[: DN_ROWS // 2, :], preferred_element_type=jnp.float32)
    even, odd = acc[:ROWS], acc[ROWS:]
    return jnp.concatenate([fold(even, odd, 0), fold(even, odd, 256)], axis=1)


def send_kernel(part_ref, weight_ref, out_ref):
    out_ref[...] = mixed_of(part_ref, weight_ref)


def own_kernel(part_ref, weight_ref, taken_ref, back_ref, taken_out, out_ref):
    taken = jnp.concatenate([taken_ref[:ROWS], taken_ref[ROWS:]], axis=1)
    taken_out[...] = jnp.dot(taken, back_ref[...], preferred_element_type=jnp.float32)
    out_ref[...] = mixed_of(part_ref, weight_ref)


def finish_kernel(taken_ref, own_ref, got_ref, order_ref, out_ref, next_ref):
    produced = (taken_ref[...] + (own_ref[...] + got_ref[...])).astype(jnp.bfloat16)
    out_ref[...] = produced
    ordered = jnp.dot(produced, order_ref[...], preferred_element_type=jnp.float32).astype(jnp.bfloat16)
    next_ref[...] = jnp.concatenate([ordered[:, :128], ordered[:, 128:]], axis=0)


def gain_kernel(norm_ref, order_ref, gain_ref, rows_ref):
    for device in range(2 * CHIPS):
        rows_ref[device : device + 1, :] = norm_ref[:, device * 256 : (device + 1) * 256]
    left = rows_ref[...]
    gain = jnp.zeros(left.shape, jnp.float32)
    for _ in range(3):
        piece = left.astype(jnp.bfloat16)
        left = left - piece.astype(jnp.float32)
        gain = gain + jnp.dot(piece, order_ref[...], preferred_element_type=jnp.float32)
    for device in range(2 * CHIPS):
        at = 2 * (device % 2 * CHIPS + device // 2)
        for p in range(2):
            gain_ref[at + p : at + p + 1, :] = gain[device : device + 1, p * 128 : (p + 1) * 128]


def prepare_kernel(x_ref, order_ref, *firsts):
    ordered = jnp.dot(x_ref[...], order_ref[...], preferred_element_type=jnp.float32).astype(jnp.bfloat16)
    for group, ref in enumerate(firsts):
        part = ordered[group * ROWS : (group + 1) * ROWS]
        ref[...] = jnp.concatenate([part[:, :128], part[:, 128:]], axis=0)


def line_kernel(at_ref, *refs):
    for shift, ref in enumerate(refs[:4]):
        refs[-1][(at_ref[0] - shift) & 3] = ref[...]


def plane_kernel(at_ref, *refs):
    for shift, ref in enumerate(refs[:4]):
        for line in range(4):
            refs[-1][line * 4 + ((at_ref[0] - shift) & 3)] = ref[line]


def pick_kernel(place_ref, *refs):
    made, out_ref = refs[:-1], refs[-1]
    groups = out_ref.shape[0] // ROWS
    for segment in range(len(made) - groups + 1):

        @pl.when(place_ref[0] == segment)
        def _():
            for group in range(groups):
                out_ref[group * ROWS : (group + 1) * ROWS, :] = made[group + segment][...]


VMEM = pl.BlockSpec(memory_space=pltpu.VMEM)
SMEM = pl.BlockSpec(memory_space=pltpu.SMEM)


def resident(weight):
    return pltpu.with_memory_space_constraint(weight, pltpu.VMEM)


def cost(products):
    return pl.CostEstimate(flops=2 * 128 * products, bytes_accessed=2 * MIB, transcendentals=0)


def prepare(x_in, x_order):
    groups = x_in.shape[0] // ROWS
    return pl.pallas_call(
        prepare_kernel,
        out_shape=[jax.ShapeDtypeStruct((2 * ROWS, 128), jnp.bfloat16)] * groups,
        in_specs=[VMEM] * 2,
        out_specs=[VMEM] * groups,
        compiler_params=pltpu.CompilerParams(vmem_limit_bytes=4 * MIB),
        name="prepare",
    )(x_in, x_order)


def gains_of(norm_gain, x_order):
    return pl.pallas_call(
        gain_kernel,
        out_shape=jax.ShapeDtypeStruct((4 * CHIPS, 128), jnp.float32),
        in_specs=[VMEM] * 2,
        out_specs=VMEM,
        scratch_shapes=[pltpu.VMEM((2 * CHIPS, 256), jnp.float32)],
        compiler_params=pltpu.CompilerParams(vmem_limit_bytes=4 * MIB),
        name="gains",
    )(norm_gain, x_order)


def placed_by(kernel, at, parts, count):
    return pl.pallas_call(
        kernel,
        out_shape=jax.ShapeDtypeStruct((count,) + parts[0].shape[-2:], parts[0].dtype),
        in_specs=[SMEM] + [VMEM] * len(parts),
        out_specs=VMEM,
        compiler_params=pltpu.CompilerParams(vmem_limit_bytes=8 * MIB),
        name="placed",
    )(at, *parts)


def shifted_all(value, along_x):
    parts = [value]
    for shift in range(1, 4):
        pairs = []
        for x in range(4):
            for y in range(4):
                goal = ((x + shift) % 4 * 4 + y) if along_x else (x * 4 + (y + shift) % 4)
                pairs += [(2 * (x * 4 + y) + core, 2 * goal + core) for core in range(2)]
        parts.append(lax.ppermute(value, "tensor", pairs))
    return parts


def call_near(core, part, gain, weight):
    return pl.pallas_call(
        near_kernel,
        out_shape=(
            jax.ShapeDtypeStruct((2 * ROWS, GU_COLS), jnp.float32),
            jax.ShapeDtypeStruct((2 * ROWS, 128), jnp.float32),
        ),
        in_specs=[SMEM, VMEM, VMEM, VMEM],
        out_specs=(VMEM, VMEM),
        scratch_shapes=[pltpu.VMEM((2 * ROWS, GU_ROWS // 2), jnp.bfloat16)],
        compiler_params=pltpu.CompilerParams(vmem_limit_bytes=16 * MIB),
        cost_estimate=cost(GU_ROWS * GU_COLS // 2),
        name="near",
    )(core, part, gain, resident(weight))


def call_far(core, part, gain, weight, order, acc, square):
    return pl.pallas_call(
        far_kernel,
        out_shape=jax.ShapeDtypeStruct((CHIPS, KEPT, 256), jnp.bfloat16),
        in_specs=[SMEM] + [VMEM] * 6,
        out_specs=VMEM,
        scratch_shapes=[pltpu.VMEM((2 * ROWS, GU_ROWS // 2), jnp.bfloat16)],
        compiler_params=pltpu.CompilerParams(vmem_limit_bytes=16 * MIB),
        cost_estimate=cost(GU_ROWS * GU_COLS // 2),
        name="far",
    )(core, part, gain, resident(weight), order, acc, square)


def call_send(part, weight):
    return pl.pallas_call(
        send_kernel,
        out_shape=jax.ShapeDtypeStruct((ROWS, 256), jnp.float32),
        in_specs=[VMEM] * 2,
        out_specs=VMEM,
        compiler_params=pltpu.CompilerParams(vmem_limit_bytes=16 * MIB),
        cost_estimate=cost(DN_ROWS * DN_COLS // 2),
        name="send",
    )(part, resident(weight))


def call_own(part, weight, taken, back):
    return pl.pallas_call(
        own_kernel,
        out_shape=[jax.ShapeDtypeStruct((ROWS, 256), jnp.float32)] * 2,
        in_specs=[VMEM] * 4,
        out_specs=[VMEM] * 2,
        compiler_params=pltpu.CompilerParams(vmem_limit_bytes=16 * MIB),
        cost_estimate=cost(DN_ROWS * DN_COLS // 2),
        name="own",
    )(part, resident(weight), taken, back)


def call_finish(taken, own, got, order):
    return pl.pallas_call(
        finish_kernel,
        out_shape=(
            jax.ShapeDtypeStruct((ROWS, 256), jnp.bfloat16),
            jax.ShapeDtypeStruct((2 * ROWS, 128), jnp.bfloat16),
        ),
        in_specs=[VMEM] * 4,
        out_specs=(VMEM, VMEM),
        compiler_params=pltpu.CompilerParams(vmem_limit_bytes=4 * MIB),
        name="finish",
    )(taken, own, got, order)


def call_pick(place, made, groups):
    return pl.pallas_call(
        pick_kernel,
        out_shape=jax.ShapeDtypeStruct((groups * ROWS, 256), jnp.bfloat16),
        in_specs=[SMEM] + [VMEM] * len(made),
        out_specs=VMEM,
        compiler_params=pltpu.CompilerParams(vmem_limit_bytes=4 * MIB),
        name="pick",
    )(place, *made)


def orders():
    source = jnp.arange(256)
    goal = (source % 2) * 128 + source // 64 * 32 + source % 64 // 2
    x_order = (goal[:, None] == jnp.arange(256)[None, :]).astype(jnp.bfloat16)
    source = jnp.arange(512)
    goal = (source % 2) * 256 + source // 64 * 32 + source % 64 // 2
    h_order = (goal[:, None] == jnp.arange(512)[None, :]).astype(jnp.bfloat16)
    return x_order, h_order


def exchanged(value):
    same_core = [[2 * chip + core for chip in range(CHIPS)] for core in range(2)]
    return lax.all_to_all(value, "tensor", 0, 0, axis_index_groups=same_core)


def swapped(value):
    return lax.ppermute(value, "tensor", [(i, i ^ 1) for i in range(2 * CHIPS)])


def local(x_in, norm_gain, in_index, gate_blocks, up_blocks, out_index, down_blocks):
    segment_count = lax.axis_size("segment")
    segment_at = lax.axis_index("segment")
    tensor_at = lax.axis_index("tensor").astype(jnp.int32)
    core = (tensor_at & 1)[None]
    tokens = x_in.shape[0]
    group_count = tokens // ROWS
    tick_count = group_count + segment_count - 1
    x_order, h_order = orders()
    x_back = x_order.T
    firsts = prepare(x_in, x_order)
    is_first = jnp.broadcast_to(segment_at == 0, (8, 128)).astype(jnp.bfloat16)
    place = segment_at.astype(jnp.int32)[None]
    x_at, y_at = (tensor_at >> 3)[None], ((tensor_at >> 1) & 3)[None]
    core, place, x_at, y_at, x_order, x_back, h_order, firsts, is_first = lax.optimization_barrier(
        (core, place, x_at, y_at, x_order, x_back, h_order, firsts, is_first)
    )

    carried = None
    made = []
    hops = [(i, i + 1) for i in range(segment_count - 1)]
    for tick in range(tick_count):
        taken = firsts[min(tick, group_count - 1)]
        if carried is not None:
            taken = jnp.where(jnp.tile(is_first, (2 * ROWS // 8, 1)) > 0, taken, carried)
        if tick == 0:
            parts = shifted_all(taken, True)
            out_now, norm_gain, core = lax.optimization_barrier((out_index[0], norm_gain, core))
            gain = gains_of(norm_gain, x_order)
            down, lent = densify_down(out_goals(out_now, core[0]), down_blocks[0])
            line = placed_by(line_kernel, x_at, parts + [resident(down), gain], 4)
            in_now, line, lent = lax.optimization_barrier((in_index[0], line, lent))
            borrowed = swapped(lent)
            parts = shifted_all(line, False)
            wide = densify_wide(in_goals(in_now), gate_blocks[0], up_blocks[0])
            mine = placed_by(plane_kernel, y_at, parts + [resident(wide)], CHIPS)
        else:
            mine = exchanged(jnp.broadcast_to(taken[None], (CHIPS, 2 * ROWS, 128)))
        other = swapped(mine)
        acc, square = call_near(core, mine, gain, wide)
        hidden = call_far(core, other, gain, wide, h_order, acc, square)
        mine = exchanged(hidden)
        got = swapped(call_send(mine, borrowed))
        residual, own = call_own(mine, down, taken, x_back)
        produced, ordered = call_finish(residual, own, got, x_order)
        made.append(produced)
        if tick + 1 < tick_count:
            carried = lax.ppermute(ordered, "segment", hops)
    return call_pick(place, made, group_count)[None]


def solution(mesh):
    placed = (
        P("replica", "tensor"),
        P("segment", None),
        P("segment", "tensor", None),
        P("segment", "tensor", None, None),
        P("segment", "tensor", None, None),
        P("segment", "tensor", None),
        P("segment", "tensor", None, None),
    )
    return jax.shard_map(
        local,
        mesh=mesh,
        in_specs=placed,
        out_specs=P("segment", "replica", "tensor"),
        check_vma=False,
    )
```

```python
import functools

import jax
import jax.numpy as jnp
from jax import lax
from jax.experimental import pallas as pl
from jax.experimental.pallas import tpu as pltpu
from jax.sharding import PartitionSpec as P

D = 8192
FFW = 14336
BS = 64
CHIPS = 16
ROWS = 64
KEPT = 112
GU_ROWS = D // 2
GU_COLS = 14 * 128
DN_ROWS = 32 * 256
DN_COLS = 4 * 128
MIB = 1 << 20


def clear(target):
    rows, cols = target.shape

    def one(at, _):
        target[pl.ds(pl.multiple_of(at * 32, 32), 32), :] = jnp.zeros((32, cols), target.dtype)
        return 0

    lax.fori_loop(0, rows // 32, one, 0)


def wide_pack_kernel(goal_ref, gate_hbm, up_hbm, target, buf, spread, sems):
    tiles, _, slots = goal_ref.shape
    for which, source in enumerate((gate_hbm, up_hbm)):
        for tile in range(tiles):
            at = which * tiles + tile
            pltpu.make_async_copy(source.at[tile], buf.at[at], sems.at[at]).start()
    clear(target)

    def place(chunk, count, first, half, tile, column):
        for group in range(0, count, 8):
            for part in range(32):
                spread[half, group * 32 + part * 8 : group * 32 + part * 8 + 8, :] = chunk[
                    group : group + 8, part * 128 : (part + 1) * 128
                ]
        for row in range(count):
            goal = pl.multiple_of(goal_ref[tile, 0, first + row], 32)
            piece = spread[half, pl.ds(row // 8 * 256 + row % 8, 32, stride=8), :]
            target[pl.ds(goal, 32), pl.ds(column, 128)] = piece.astype(target.dtype)

    def one(at, _):
        pltpu.make_async_copy(gate_hbm.at[0], buf.at[at], sems.at[at]).wait()
        which = (at >= tiles).astype(jnp.int32)
        tile = at - which * tiles
        last = tiles - 1
        column = pl.multiple_of(jnp.where(tile == last, 2 * last + which, which * last + tile) * 128, 128)

        def pair(step, _):
            for half in range(2):
                first = pl.multiple_of(step * 32 + half * 16, 16)
                chunk = buf[at, pl.ds(first, 16), :].astype(jnp.float32)
                place(chunk, 16, first, half, tile, column)
            return 0

        lax.fori_loop(0, slots // 32, pair, 0)
        done = slots // 32 * 32
        half = 0
        while done < slots:
            count = min(16, slots - done)
            chunk = buf[at, done : done + count, :].astype(jnp.float32)
            place(chunk, count, done, half, tile, column)
            done += count
            half = 1 - half
        return 0

    lax.fori_loop(0, 2 * tiles, one, 0)


def down_pack_kernel(goal_ref, source, near, far, buf, spread, sems):
    _, tiles, slots = goal_ref.shape
    parts = 7
    size = slots // parts
    for part in range(parts):
        pltpu.make_async_copy(
            source.at[pl.ds(part * size, size)], buf.at[pl.ds(part * size, size)], sems.at[part]
        ).start()
    clear(near)
    clear(far)

    def one(part, _):
        pltpu.make_async_copy(
            source.at[pl.ds(0, size)], buf.at[pl.ds(part * size, size)], sems.at[part]
        ).wait()

        def step(at, _):
            for half in range(3):
                slot = part * size + at * 6 + half * 2
                for inner in range(2):
                    chunk = buf[slot + inner].astype(jnp.float32)
                    for lane in range(32):
                        spread[half, lane * 8 + inner * 4 : lane * 8 + inner * 4 + 4, :] = chunk[
                            :, lane * 128 : (lane + 1) * 128
                        ]
                for inner in range(2):
                    for tile in range(tiles):
                        piece = spread[half, pl.ds(inner * 4 + tile, 32, stride=8), :].astype(near.dtype)
                        for side, target in enumerate((near, far)):
                            goal = pl.multiple_of(goal_ref[side, tile, slot + inner], 32)
                            target[pl.ds(goal, 32), tile * 128 : (tile + 1) * 128] = piece
            return 0

        lax.fori_loop(0, size // 6, step, 0)
        return 0

    lax.fori_loop(0, parts, one, 0)


def pack(kernel, goals, sources, buf, spread, copies, shape, results, name):
    sources = [pltpu.with_memory_space_constraint(source, pltpu.HBM) for source in sources]
    return pl.pallas_call(
        kernel,
        out_shape=[pltpu.VMEM(shape, jnp.bfloat16)] * results,
        in_specs=[pl.BlockSpec(memory_space=pltpu.SMEM)]
        + [pl.BlockSpec(memory_space=pltpu.HBM)] * len(sources),
        out_specs=[pl.BlockSpec(memory_space=pltpu.VMEM)] * results,
        scratch_shapes=[
            pltpu.VMEM(buf, jnp.bfloat16),
            pltpu.VMEM(spread + (128,), jnp.float32),
            pltpu.SemaphoreType.DMA((copies,)),
        ],
        compiler_params=pltpu.CompilerParams(vmem_limit_bytes=12 * MIB),
        cost_estimate=pl.CostEstimate(flops=0, bytes_accessed=40 * MIB, transcendentals=0),
        name=name,
    )(goals, *sources)


def densify_wide(goals, gate_blocks, up_blocks):
    tiles, _, slots = goals.shape
    buf = (2 * tiles, slots, BS * BS)
    shape = (GU_ROWS + 32, GU_COLS)
    sources = (gate_blocks, up_blocks)
    return pack(wide_pack_kernel, goals, sources, buf, (2, 512), 2 * tiles, shape, 1, "pack_wide")[0]


def densify_down(goals, blocks):
    tiles, slots = blocks.shape[:2]
    shape = (DN_ROWS // 2 + 32, DN_COLS)
    blocks = jnp.transpose(blocks, (1, 0, 2))
    buf = (slots, tiles, BS * BS)
    return pack(down_pack_kernel, goals, (blocks,), buf, (3, 256), 7, shape, 2, "pack_down")


def in_goals(index):
    row = (((index >> 2) & 1) * CHIPS + (index >> 3)) * 128 + (index & 3) * 32
    return jnp.where(index >= 0, row, GU_ROWS)


def out_goals(index, core):
    device = (index * 9363) >> 16
    row = (device >> 1) * 256 + (index - device * 7) * 32
    near = (device & 1) == core
    trash = DN_ROWS // 2
    near_row = jnp.where(near, row, trash)
    far_row = jnp.where(near, trash, row)
    return jnp.where(index >= 0, near_row, trash), jnp.where(index >= 0, far_row, trash)


def fold(even, odd, at):
    low = lax.broadcasted_iota(jnp.int32, (ROWS, 128), 1) < 64
    e0, e1 = even[:, at : at + 128], even[:, at + 128 : at + 256]
    o0, o1 = odd[:, at : at + 128], odd[:, at + 128 : at + 256]
    return jnp.where(low, e0, o1) + pltpu.roll(jnp.where(low, e1, o0), 64, 1)


def near_kernel(core_ref, part_ref, gain_ref, weight_ref, acc_ref, square_ref, scaled):
    core = core_ref[0]
    total = jnp.zeros((2 * ROWS, 128), jnp.float32)
    gains = gain_ref[pl.ds(pl.multiple_of(core * 32, 32), 32), :]
    for chip in range(CHIPS):
        value = part_ref[chip].astype(jnp.float32)
        total += value * value
        scaled[:, chip * 128 : (chip + 1) * 128] = (value * both_rows(gains, chip)).astype(jnp.bfloat16)
    square_ref[...] = total
    rows = pl.ds(pl.multiple_of(core * (GU_ROWS // 2), GU_ROWS // 2), GU_ROWS // 2)
    for tile in range(7):
        acc_ref[:, tile * 256 : (tile + 1) * 256] = jnp.dot(
            scaled[...], weight_ref[rows, tile * 256 : (tile + 1) * 256], preferred_element_type=jnp.float32
        )


def both_rows(gains, chip):
    return jnp.concatenate(
        [jnp.broadcast_to(gains[2 * chip + p : 2 * chip + p + 1], (ROWS, 128)) for p in range(2)], axis=0
    )


def far_kernel(core_ref, part_ref, gain_ref, weight_ref, order_ref, acc_ref, square_ref, out_ref, scaled):
    core = 1 - core_ref[0]
    total = square_ref[...]
    gains = gain_ref[pl.ds(pl.multiple_of(core * 32, 32), 32), :]
    for chip in range(CHIPS):
        value = part_ref[chip].astype(jnp.float32)
        total += value * value
        scaled[:, chip * 128 : (chip + 1) * 128] = (value * both_rows(gains, chip)).astype(jnp.bfloat16)
    stat = jnp.sum(total[:ROWS] + total[ROWS:], axis=1, keepdims=True) / D
    scale = lax.rsqrt(stat + 1e-05)
    rows = pl.ds(pl.multiple_of(core * (GU_ROWS // 2), GU_ROWS // 2), GU_ROWS // 2)

    def product(tile):
        acc = acc_ref[:, tile * 256 : (tile + 1) * 256] + jnp.dot(
            scaled[...], weight_ref[rows, tile * 256 : (tile + 1) * 256], preferred_element_type=jnp.float32
        )
        return fold(acc[:ROWS], acc[ROWS:], 0) * scale

    pieces = []
    for pair in range(3):
        gate = product(pair)
        up = product(pair + 3)
        pieces.append((gate / (1.0 + jnp.exp(-gate)) * up).astype(jnp.bfloat16))
    both = product(6)
    last = both / (1.0 + jnp.exp(-both)) * pltpu.roll(both, 64, 1)
    low = lax.broadcasted_iota(jnp.int32, (ROWS, 128), 1) < 64
    pieces.append(jnp.where(low, last, 0.0).astype(jnp.bfloat16))
    hidden = jnp.dot(
        jnp.concatenate(pieces, axis=1), order_ref[...], preferred_element_type=jnp.float32
    )
    hidden = jnp.concatenate([hidden[:, :256], hidden[:, 256:]], axis=0)
    extra = []
    for slot in range(7):
        half = slot // 4 * 128
        piece = hidden[KEPT:, half : half + 128]
        extra.append(pltpu.roll(piece, (96 - slot % 4 * 32) % 128, 1) if slot % 4 != 3 else piece)
    spare = lax.broadcasted_iota(jnp.int32, (KEPT, 128), 1) >= 96
    right = jnp.where(spare, jnp.concatenate(extra, axis=0), hidden[:KEPT, 128:])
    hidden = jnp.concatenate([hidden[:KEPT, :128], right], axis=1).astype(jnp.bfloat16)
    for chip in range(CHIPS):
        out_ref[chip] = hidden


def mixed_of(part_ref, weight_ref):
    lane = lax.broadcasted_iota(jnp.int32, (16, 128), 1)
    pieces = []
    for chip in range(CHIPS):
        tails = []
        for half in range(2):
            tail = jnp.zeros((16, 128), jnp.float32)
            for slot in range(half * 4, min(half * 4 + 4, 7)):
                piece = part_ref[chip, slot * 16 : slot * 16 + 16, 128:].astype(jnp.float32)
                at = slot % 4 * 32
                piece = pltpu.roll(piece, (at + 32) % 128, 1) if at != 96 else piece
                tail = jnp.where((lane >= at) & (lane < at + 32), piece, tail)
            tails.append(tail)
        tail = jnp.concatenate(tails, axis=1).astype(jnp.bfloat16)
        pieces.append(jnp.concatenate([part_ref[chip], tail], axis=0))
    left = jnp.concatenate(pieces, axis=1)
    acc = jnp.dot(left, weight_ref[: DN_ROWS // 2, :], preferred_element_type=jnp.float32)
    even, odd = acc[:ROWS], acc[ROWS:]
    return jnp.concatenate([fold(even, odd, 0), fold(even, odd, 256)], axis=1)


def send_kernel(part_ref, weight_ref, out_ref):
    out_ref[...] = mixed_of(part_ref, weight_ref)


def own_kernel(part_ref, weight_ref, taken_ref, back_ref, taken_out, out_ref):
    taken = jnp.concatenate([taken_ref[:ROWS], taken_ref[ROWS:]], axis=1)
    taken_out[...] = jnp.dot(taken, back_ref[...], preferred_element_type=jnp.float32)
    out_ref[...] = mixed_of(part_ref, weight_ref)


def finish_kernel(taken_ref, own_ref, got_ref, order_ref, out_ref, next_ref):
    produced = (taken_ref[...] + (own_ref[...] + got_ref[...])).astype(jnp.bfloat16)
    out_ref[...] = produced
    ordered = jnp.dot(produced, order_ref[...], preferred_element_type=jnp.float32).astype(jnp.bfloat16)
    next_ref[...] = jnp.concatenate([ordered[:, :128], ordered[:, 128:]], axis=0)


def prepare_kernel(groups, core_ref, x_hbm, norm_hbm, in_hbm, out_hbm, order_ref, *refs):
    firsts = refs[:groups]
    gain_ref, wide_goal, down_goal, x_ref, norm_ref, in_ref, out_ref, rows_ref, sems = refs[groups:]
    pairs = ((x_hbm, x_ref), (norm_hbm, norm_ref), (in_hbm, in_ref), (out_hbm, out_ref))
    copies = [pltpu.make_async_copy(a, b, sems.at[at]) for at, (a, b) in enumerate(pairs)]
    for copy in copies:
        copy.start()
    for copy in copies:
        copy.wait()
    ordered = jnp.dot(x_ref[...], order_ref[...], preferred_element_type=jnp.float32).astype(jnp.bfloat16)
    for group, ref in enumerate(firsts):
        part = ordered[group * ROWS : (group + 1) * ROWS]
        ref[...] = jnp.concatenate([part[:, :128], part[:, 128:]], axis=0)
    for device in range(2 * CHIPS):
        rows_ref[device : device + 1, :] = norm_ref[:, device * 256 : (device + 1) * 256]
    left = rows_ref[...]
    gain = jnp.zeros(left.shape, jnp.float32)
    for _ in range(3):
        piece = left.astype(jnp.bfloat16)
        left = left - piece.astype(jnp.float32)
        gain = gain + jnp.dot(piece, order_ref[...], preferred_element_type=jnp.float32)
    for device in range(2 * CHIPS):
        at = 2 * (device % 2 * CHIPS + device // 2)
        for p in range(2):
            gain_ref[at + p : at + p + 1, :] = gain[device : device + 1, p * 128 : (p + 1) * 128]
    wide_goal[...] = in_goals(in_ref[...])
    near, far = out_goals(out_ref[...], core_ref[0])
    down_goal[0] = near
    down_goal[1] = far


def line_kernel(at_ref, *refs):
    for shift, ref in enumerate(refs[:4]):
        refs[-1][(at_ref[0] - shift) & 3] = ref[...]


def plane_kernel(at_ref, *refs):
    for shift, ref in enumerate(refs[:4]):
        for line in range(4):
            refs[-1][line * 4 + ((at_ref[0] - shift) & 3)] = ref[line]


def last_kernel(place_ref, taken_ref, own_ref, got_ref, *refs):
    made, out_ref = refs[:-1], refs[-1]
    groups = out_ref.shape[0] // ROWS
    for segment in range(len(made) - groups + 1):

        @pl.when(place_ref[0] == segment)
        def _():
            for group in range(groups):
                out_ref[group * ROWS : (group + 1) * ROWS, :] = made[group + segment][...]

    @pl.when(place_ref[0] == len(made) - groups + 1)
    def _():
        for group in range(groups - 1):
            at = len(made) - groups + 1 + group
            out_ref[group * ROWS : (group + 1) * ROWS, :] = made[at][...]
        produced = (taken_ref[...] + (own_ref[...] + got_ref[...])).astype(jnp.bfloat16)
        out_ref[(groups - 1) * ROWS :, :] = produced


VMEM = pl.BlockSpec(memory_space=pltpu.VMEM)
SMEM = pl.BlockSpec(memory_space=pltpu.SMEM)


def resident(weight):
    return pltpu.with_memory_space_constraint(weight, pltpu.VMEM)


def cost(products):
    return pl.CostEstimate(flops=2 * 128 * products, bytes_accessed=2 * MIB, transcendentals=0)


def prepare(core, x_in, norm_gain, in_index, out_index, x_order):
    groups = x_in.shape[0] // ROWS
    hbm = [pltpu.with_memory_space_constraint(v, pltpu.HBM) for v in (x_in, norm_gain, in_index, out_index)]
    return pl.pallas_call(
        functools.partial(prepare_kernel, groups),
        out_shape=[jax.ShapeDtypeStruct((2 * ROWS, 128), jnp.bfloat16)] * groups
        + [
            jax.ShapeDtypeStruct((4 * CHIPS, 128), jnp.float32),
            jax.ShapeDtypeStruct(in_index.shape, jnp.int32),
            jax.ShapeDtypeStruct((2,) + out_index.shape, jnp.int32),
        ],
        in_specs=[SMEM] + [pl.BlockSpec(memory_space=pltpu.HBM)] * 4 + [VMEM],
        out_specs=[VMEM] * (groups + 3),
        scratch_shapes=[pltpu.VMEM(v.shape, v.dtype) for v in (x_in, norm_gain, in_index, out_index)]
        + [pltpu.VMEM((2 * CHIPS, 256), jnp.float32), pltpu.SemaphoreType.DMA((4,))],
        compiler_params=pltpu.CompilerParams(vmem_limit_bytes=4 * MIB),
        name="prepare",
    )(core, *hbm, x_order)


def placed_by(kernel, at, parts, count):
    return pl.pallas_call(
        kernel,
        out_shape=jax.ShapeDtypeStruct((count,) + parts[0].shape[-2:], parts[0].dtype),
        in_specs=[SMEM] + [VMEM] * len(parts),
        out_specs=VMEM,
        compiler_params=pltpu.CompilerParams(vmem_limit_bytes=8 * MIB),
        name="placed",
    )(at, *parts)


def shifted_all(value, along_x):
    parts = [value]
    for shift in range(1, 4):
        pairs = []
        for x in range(4):
            for y in range(4):
                goal = ((x + shift) % 4 * 4 + y) if along_x else (x * 4 + (y + shift) % 4)
                pairs += [(2 * (x * 4 + y) + core, 2 * goal + core) for core in range(2)]
        parts.append(lax.ppermute(value, "tensor", pairs))
    return parts


def call_near(core, part, gain, weight):
    return pl.pallas_call(
        near_kernel,
        out_shape=(
            jax.ShapeDtypeStruct((2 * ROWS, GU_COLS), jnp.float32),
            jax.ShapeDtypeStruct((2 * ROWS, 128), jnp.float32),
        ),
        in_specs=[SMEM, VMEM, VMEM, VMEM],
        out_specs=(VMEM, VMEM),
        scratch_shapes=[pltpu.VMEM((2 * ROWS, GU_ROWS // 2), jnp.bfloat16)],
        compiler_params=pltpu.CompilerParams(vmem_limit_bytes=16 * MIB),
        cost_estimate=cost(GU_ROWS * GU_COLS // 2),
        name="near",
    )(core, part, gain, resident(weight))


def call_far(core, part, gain, weight, order, acc, square):
    return pl.pallas_call(
        far_kernel,
        out_shape=jax.ShapeDtypeStruct((CHIPS, KEPT, 256), jnp.bfloat16),
        in_specs=[SMEM] + [VMEM] * 6,
        out_specs=VMEM,
        scratch_shapes=[pltpu.VMEM((2 * ROWS, GU_ROWS // 2), jnp.bfloat16)],
        compiler_params=pltpu.CompilerParams(vmem_limit_bytes=16 * MIB),
        cost_estimate=cost(GU_ROWS * GU_COLS // 2),
        name="far",
    )(core, part, gain, resident(weight), order, acc, square)


def call_send(part, weight):
    return pl.pallas_call(
        send_kernel,
        out_shape=jax.ShapeDtypeStruct((ROWS, 256), jnp.float32),
        in_specs=[VMEM] * 2,
        out_specs=VMEM,
        compiler_params=pltpu.CompilerParams(vmem_limit_bytes=16 * MIB),
        cost_estimate=cost(DN_ROWS * DN_COLS // 2),
        name="send",
    )(part, resident(weight))


def call_own(part, weight, taken, back):
    return pl.pallas_call(
        own_kernel,
        out_shape=[jax.ShapeDtypeStruct((ROWS, 256), jnp.float32)] * 2,
        in_specs=[VMEM] * 4,
        out_specs=[VMEM] * 2,
        compiler_params=pltpu.CompilerParams(vmem_limit_bytes=16 * MIB),
        cost_estimate=cost(DN_ROWS * DN_COLS // 2),
        name="own",
    )(part, resident(weight), taken, back)


def call_finish(taken, own, got, order):
    return pl.pallas_call(
        finish_kernel,
        out_shape=(
            jax.ShapeDtypeStruct((ROWS, 256), jnp.bfloat16),
            jax.ShapeDtypeStruct((2 * ROWS, 128), jnp.bfloat16),
        ),
        in_specs=[VMEM] * 4,
        out_specs=(VMEM, VMEM),
        compiler_params=pltpu.CompilerParams(vmem_limit_bytes=4 * MIB),
        name="finish",
    )(taken, own, got, order)


def call_last(place, taken, own, got, made, groups):
    return pl.pallas_call(
        last_kernel,
        out_shape=jax.ShapeDtypeStruct((groups * ROWS, 256), jnp.bfloat16),
        in_specs=[SMEM] + [VMEM] * (3 + len(made)),
        out_specs=VMEM,
        compiler_params=pltpu.CompilerParams(vmem_limit_bytes=4 * MIB),
        name="last",
    )(place, taken, own, got, *made)


def orders():
    source = jnp.arange(256)
    goal = (source % 2) * 128 + source // 64 * 32 + source % 64 // 2
    x_order = (goal[:, None] == jnp.arange(256)[None, :]).astype(jnp.bfloat16)
    source = jnp.arange(512)
    goal = (source % 2) * 256 + source // 64 * 32 + source % 64 // 2
    h_order = (goal[:, None] == jnp.arange(512)[None, :]).astype(jnp.bfloat16)
    return x_order, h_order


def exchanged(value):
    same_core = [[2 * chip + core for chip in range(CHIPS)] for core in range(2)]
    return lax.all_to_all(value, "tensor", 0, 0, axis_index_groups=same_core)


def swapped(value):
    return lax.ppermute(value, "tensor", [(i, i ^ 1) for i in range(2 * CHIPS)])


def local(x_in, norm_gain, in_index, gate_blocks, up_blocks, out_index, down_blocks):
    segment_count = lax.axis_size("segment")
    segment_at = lax.axis_index("segment")
    tensor_at = lax.axis_index("tensor").astype(jnp.int32)
    core = (tensor_at & 1)[None]
    tokens = x_in.shape[0]
    group_count = tokens // ROWS
    tick_count = group_count + segment_count - 1
    x_order, h_order = orders()
    x_back = x_order.T
    in_index = jnp.transpose(in_index, (1, 0, 2))
    *firsts, gain, to_wide, to_down = prepare(core, x_in, norm_gain, in_index, out_index[0], x_order)
    is_first = jnp.broadcast_to(segment_at == 0, (8, 128)).astype(jnp.bfloat16)
    place = segment_at.astype(jnp.int32)[None]
    x_at, y_at = (tensor_at >> 3)[None], ((tensor_at >> 1) & 3)[None]
    core, place, x_at, y_at, x_order, x_back, h_order, firsts, gain, is_first = lax.optimization_barrier(
        (core, place, x_at, y_at, x_order, x_back, h_order, firsts, gain, is_first)
    )

    carried = None
    made = []
    hops = [(i, i + 1) for i in range(segment_count - 1)]
    for tick in range(tick_count):
        taken = firsts[min(tick, group_count - 1)]
        if carried is not None:
            taken = jnp.where(jnp.tile(is_first, (2 * ROWS // 8, 1)) > 0, taken, carried)
        if tick == 0:
            parts = shifted_all(taken, True)
            down, lent = densify_down(to_down, down_blocks[0])
            line = placed_by(line_kernel, x_at, parts + [resident(down)], 4)
            to_wide, line, lent = lax.optimization_barrier((to_wide, line, lent))
            borrowed = swapped(lent)
            parts = shifted_all(line, False)
            wide = densify_wide(to_wide, gate_blocks[0], up_blocks[0])
            mine = placed_by(plane_kernel, y_at, parts + [resident(wide)], CHIPS)
        else:
            mine = exchanged(jnp.broadcast_to(taken[None], (CHIPS, 2 * ROWS, 128)))
        other = swapped(mine)
        acc, square = call_near(core, mine, gain, wide)
        hidden = call_far(core, other, gain, wide, h_order, acc, square)
        mine = exchanged(hidden)
        got = swapped(call_send(mine, borrowed))
        residual, own = call_own(mine, down, taken, x_back)
        if tick + 1 == tick_count:
            return call_last(place, residual, own, got, made, group_count)[None]
        produced, ordered = call_finish(residual, own, got, x_order)
        made.append(produced)
        carried = lax.ppermute(ordered, "segment", hops)


def solution(mesh):
    placed = (
        P("replica", "tensor"),
        P("segment", None),
        P("segment", "tensor", None),
        P("segment", "tensor", None, None),
        P("segment", "tensor", None, None),
        P("segment", "tensor", None),
        P("segment", "tensor", None, None),
    )
    return jax.shard_map(
        local,
        mesh=mesh,
        in_specs=placed,
        out_specs=P("segment", "replica", "tensor"),
        check_vma=False,
    )
```

```python
import functools

import jax
import jax.numpy as jnp
from jax import lax
from jax.experimental import pallas as pl
from jax.experimental.pallas import tpu as pltpu
from jax.sharding import PartitionSpec as P

D = 8192
FFW = 14336
BS = 64
CHIPS = 16
ROWS = 64
KEPT = 112
GU_ROWS = D // 2
GU_COLS = 14 * 128
DN_ROWS = 32 * 256
DN_COLS = 4 * 128
MIB = 1 << 20


def clear(target):
    rows, cols = target.shape

    def one(at, _):
        target[pl.ds(pl.multiple_of(at * 32, 32), 32), :] = jnp.zeros((32, cols), target.dtype)
        return 0

    lax.fori_loop(0, rows // 32, one, 0)


def wide_pack_kernel(goal_ref, gate_hbm, up_hbm, target, buf, spread, sems):
    tiles, _, slots = goal_ref.shape
    for which, source in enumerate((gate_hbm, up_hbm)):
        for tile in range(tiles):
            at = which * tiles + tile
            pltpu.make_async_copy(source.at[tile], buf.at[at], sems.at[at]).start()
    clear(target)

    def place(chunk, count, first, half, tile, column):
        for group in range(0, count, 8):
            for part in range(32):
                spread[half, group * 32 + part * 8 : group * 32 + part * 8 + 8, :] = chunk[
                    group : group + 8, part * 128 : (part + 1) * 128
                ]
        for row in range(count):
            goal = pl.multiple_of(goal_ref[tile, 0, first + row], 32)
            piece = spread[half, pl.ds(row // 8 * 256 + row % 8, 32, stride=8), :]
            target[pl.ds(goal, 32), pl.ds(column, 128)] = piece.astype(target.dtype)

    def one(at, _):
        pltpu.make_async_copy(gate_hbm.at[0], buf.at[at], sems.at[at]).wait()
        which = (at >= tiles).astype(jnp.int32)
        tile = at - which * tiles
        last = tiles - 1
        column = pl.multiple_of(jnp.where(tile == last, 2 * last + which, which * last + tile) * 128, 128)

        def pair(step, _):
            for half in range(2):
                first = pl.multiple_of(step * 32 + half * 16, 16)
                chunk = buf[at, pl.ds(first, 16), :].astype(jnp.float32)
                place(chunk, 16, first, half, tile, column)
            return 0

        lax.fori_loop(0, slots // 32, pair, 0, unroll=True)
        done = slots // 32 * 32
        half = 0
        while done < slots:
            count = min(16, slots - done)
            chunk = buf[at, done : done + count, :].astype(jnp.float32)
            place(chunk, count, done, half, tile, column)
            done += count
            half = 1 - half
        return 0

    lax.fori_loop(0, 2 * tiles, one, 0)


def down_pack_kernel(goal_ref, source, near, far, buf, spread, sems):
    _, tiles, slots = goal_ref.shape
    parts = 7
    size = slots // parts
    for part in range(parts):
        pltpu.make_async_copy(
            source.at[pl.ds(part * size, size)], buf.at[pl.ds(part * size, size)], sems.at[part]
        ).start()
    clear(near)
    clear(far)

    def one(part, _):
        pltpu.make_async_copy(
            source.at[pl.ds(0, size)], buf.at[pl.ds(part * size, size)], sems.at[part]
        ).wait()

        def step(at, _):
            for half in range(3):
                slot = part * size + at * 6 + half * 2
                for inner in range(2):
                    chunk = buf[slot + inner].astype(jnp.float32)
                    for lane in range(32):
                        spread[half, lane * 8 + inner * 4 : lane * 8 + inner * 4 + 4, :] = chunk[
                            :, lane * 128 : (lane + 1) * 128
                        ]
                for inner in range(2):
                    for tile in range(tiles):
                        piece = spread[half, pl.ds(inner * 4 + tile, 32, stride=8), :].astype(near.dtype)
                        for side, target in enumerate((near, far)):
                            goal = pl.multiple_of(goal_ref[side, tile, slot + inner], 32)
                            target[pl.ds(goal, 32), tile * 128 : (tile + 1) * 128] = piece
            return 0

        lax.fori_loop(0, size // 6, step, 0, unroll=True)
        return 0

    lax.fori_loop(0, parts, one, 0)


def pack(kernel, goals, sources, buf, spread, copies, shape, results, name):
    sources = [pltpu.with_memory_space_constraint(source, pltpu.HBM) for source in sources]
    return pl.pallas_call(
        kernel,
        out_shape=[pltpu.VMEM(shape, jnp.bfloat16)] * results,
        in_specs=[pl.BlockSpec(memory_space=pltpu.SMEM)]
        + [pl.BlockSpec(memory_space=pltpu.HBM)] * len(sources),
        out_specs=[pl.BlockSpec(memory_space=pltpu.VMEM)] * results,
        scratch_shapes=[
            pltpu.VMEM(buf, jnp.bfloat16),
            pltpu.VMEM(spread + (128,), jnp.float32),
            pltpu.SemaphoreType.DMA((copies,)),
        ],
        compiler_params=pltpu.CompilerParams(vmem_limit_bytes=12 * MIB),
        cost_estimate=pl.CostEstimate(flops=0, bytes_accessed=40 * MIB, transcendentals=0),
        name=name,
    )(goals, *sources)


def densify_wide(goals, gate_blocks, up_blocks):
    tiles, _, slots = goals.shape
    buf = (2 * tiles, slots, BS * BS)
    shape = (GU_ROWS + 32, GU_COLS)
    sources = (gate_blocks, up_blocks)
    return pack(wide_pack_kernel, goals, sources, buf, (2, 512), 2 * tiles, shape, 1, "pack_wide")[0]


def densify_down(goals, blocks):
    tiles, slots = blocks.shape[:2]
    shape = (DN_ROWS // 2 + 32, DN_COLS)
    blocks = jnp.transpose(blocks, (1, 0, 2))
    buf = (slots, tiles, BS * BS)
    return pack(down_pack_kernel, goals, (blocks,), buf, (3, 256), 7, shape, 2, "pack_down")


def in_goals(index):
    row = (((index >> 2) & 1) * CHIPS + (index >> 3)) * 128 + (index & 3) * 32
    return jnp.where(index >= 0, row, GU_ROWS)


def out_goals(index, core):
    device = (index * 9363) >> 16
    row = (device >> 1) * 256 + (index - device * 7) * 32
    near = (device & 1) == core
    trash = DN_ROWS // 2
    near_row = jnp.where(near, row, trash)
    far_row = jnp.where(near, trash, row)
    return jnp.where(index >= 0, near_row, trash), jnp.where(index >= 0, far_row, trash)


def fold(even, odd, at):
    low = lax.broadcasted_iota(jnp.int32, (ROWS, 128), 1) < 64
    e0, e1 = even[:, at : at + 128], even[:, at + 128 : at + 256]
    o0, o1 = odd[:, at : at + 128], odd[:, at + 128 : at + 256]
    return jnp.where(low, e0, o1) + pltpu.roll(jnp.where(low, e1, o0), 64, 1)


def near_kernel(core_ref, part_ref, gain_ref, weight_ref, acc_ref, square_ref, scaled):
    core = core_ref[0]
    total = jnp.zeros((2 * ROWS, 128), jnp.float32)
    gains = gain_ref[pl.ds(pl.multiple_of(core * 32, 32), 32), :]
    for chip in range(CHIPS):
        value = part_ref[chip].astype(jnp.float32)
        total += value * value
        scaled[:, chip * 128 : (chip + 1) * 128] = (value * both_rows(gains, chip)).astype(jnp.bfloat16)
    square_ref[...] = total
    rows = pl.ds(pl.multiple_of(core * (GU_ROWS // 2), GU_ROWS // 2), GU_ROWS // 2)
    for tile in range(7):
        acc_ref[:, tile * 256 : (tile + 1) * 256] = jnp.dot(
            scaled[...], weight_ref[rows, tile * 256 : (tile + 1) * 256], preferred_element_type=jnp.float32
        )


def both_rows(gains, chip):
    return jnp.concatenate(
        [jnp.broadcast_to(gains[2 * chip + p : 2 * chip + p + 1], (ROWS, 128)) for p in range(2)], axis=0
    )


def far_kernel(core_ref, part_ref, gain_ref, weight_ref, order_ref, acc_ref, square_ref, out_ref, scaled):
    core = 1 - core_ref[0]
    total = square_ref[...]
    gains = gain_ref[pl.ds(pl.multiple_of(core * 32, 32), 32), :]
    for chip in range(CHIPS):
        value = part_ref[chip].astype(jnp.float32)
        total += value * value
        scaled[:, chip * 128 : (chip + 1) * 128] = (value * both_rows(gains, chip)).astype(jnp.bfloat16)
    stat = jnp.sum(total[:ROWS] + total[ROWS:], axis=1, keepdims=True) / D
    scale = lax.rsqrt(stat + 1e-05)
    rows = pl.ds(pl.multiple_of(core * (GU_ROWS // 2), GU_ROWS // 2), GU_ROWS // 2)

    def product(tile):
        acc = acc_ref[:, tile * 256 : (tile + 1) * 256] + jnp.dot(
            scaled[...], weight_ref[rows, tile * 256 : (tile + 1) * 256], preferred_element_type=jnp.float32
        )
        return fold(acc[:ROWS], acc[ROWS:], 0) * scale

    pieces = []
    for pair in range(3):
        gate = product(pair)
        up = product(pair + 3)
        pieces.append((gate / (1.0 + jnp.exp(-gate)) * up).astype(jnp.bfloat16))
    both = product(6)
    last = both / (1.0 + jnp.exp(-both)) * pltpu.roll(both, 64, 1)
    low = lax.broadcasted_iota(jnp.int32, (ROWS, 128), 1) < 64
    pieces.append(jnp.where(low, last, 0.0).astype(jnp.bfloat16))
    hidden = jnp.dot(
        jnp.concatenate(pieces, axis=1), order_ref[...], preferred_element_type=jnp.float32
    )
    hidden = jnp.concatenate([hidden[:, :256], hidden[:, 256:]], axis=0)
    extra = []
    for slot in range(7):
        half = slot // 4 * 128
        piece = hidden[KEPT:, half : half + 128]
        extra.append(pltpu.roll(piece, (96 - slot % 4 * 32) % 128, 1) if slot % 4 != 3 else piece)
    spare = lax.broadcasted_iota(jnp.int32, (KEPT, 128), 1) >= 96
    right = jnp.where(spare, jnp.concatenate(extra, axis=0), hidden[:KEPT, 128:])
    hidden = jnp.concatenate([hidden[:KEPT, :128], right], axis=1).astype(jnp.bfloat16)
    for chip in range(CHIPS):
        out_ref[chip] = hidden


def mixed_of(part_ref, weight_ref):
    lane = lax.broadcasted_iota(jnp.int32, (16, 128), 1)
    pieces = []
    for chip in range(CHIPS):
        tails = []
        for half in range(2):
            tail = jnp.zeros((16, 128), jnp.float32)
            for slot in range(half * 4, min(half * 4 + 4, 7)):
                piece = part_ref[chip, slot * 16 : slot * 16 + 16, 128:].astype(jnp.float32)
                at = slot % 4 * 32
                piece = pltpu.roll(piece, (at + 32) % 128, 1) if at != 96 else piece
                tail = jnp.where((lane >= at) & (lane < at + 32), piece, tail)
            tails.append(tail)
        tail = jnp.concatenate(tails, axis=1).astype(jnp.bfloat16)
        pieces.append(jnp.concatenate([part_ref[chip], tail], axis=0))
    left = jnp.concatenate(pieces, axis=1)
    acc = jnp.dot(left, weight_ref[: DN_ROWS // 2, :], preferred_element_type=jnp.float32)
    even, odd = acc[:ROWS], acc[ROWS:]
    return jnp.concatenate([fold(even, odd, 0), fold(even, odd, 256)], axis=1)


def send_kernel(part_ref, weight_ref, out_ref):
    out_ref[...] = mixed_of(part_ref, weight_ref)


def own_kernel(part_ref, weight_ref, taken_ref, back_ref, taken_out, out_ref):
    taken = jnp.concatenate([taken_ref[:ROWS], taken_ref[ROWS:]], axis=1)
    taken_out[...] = jnp.dot(taken, back_ref[...], preferred_element_type=jnp.float32)
    out_ref[...] = mixed_of(part_ref, weight_ref)


def finish_kernel(taken_ref, own_ref, got_ref, order_ref, out_ref, next_ref):
    produced = (taken_ref[...] + (own_ref[...] + got_ref[...])).astype(jnp.bfloat16)
    out_ref[...] = produced
    ordered = jnp.dot(produced, order_ref[...], preferred_element_type=jnp.float32).astype(jnp.bfloat16)
    next_ref[...] = jnp.concatenate([ordered[:, :128], ordered[:, 128:]], axis=0)


def prepare_kernel(groups, core_ref, x_hbm, norm_hbm, in_hbm, out_hbm, order_ref, *refs):
    firsts = refs[:groups]
    gain_ref, wide_goal, down_goal, x_ref, norm_ref, in_ref, out_ref, rows_ref, sems = refs[groups:]
    pairs = ((x_hbm, x_ref), (norm_hbm, norm_ref), (in_hbm, in_ref), (out_hbm, out_ref))
    copies = [pltpu.make_async_copy(a, b, sems.at[at]) for at, (a, b) in enumerate(pairs)]
    for copy in copies:
        copy.start()
    for copy in copies:
        copy.wait()
    ordered = jnp.dot(x_ref[...], order_ref[...], preferred_element_type=jnp.float32).astype(jnp.bfloat16)
    for group, ref in enumerate(firsts):
        part = ordered[group * ROWS : (group + 1) * ROWS]
        ref[...] = jnp.concatenate([part[:, :128], part[:, 128:]], axis=0)
    for device in range(2 * CHIPS):
        rows_ref[device : device + 1, :] = norm_ref[:, device * 256 : (device + 1) * 256]
    left = rows_ref[...]
    gain = jnp.zeros(left.shape, jnp.float32)
    for _ in range(3):
        piece = left.astype(jnp.bfloat16)
        left = left - piece.astype(jnp.float32)
        gain = gain + jnp.dot(piece, order_ref[...], preferred_element_type=jnp.float32)
    for device in range(2 * CHIPS):
        at = 2 * (device % 2 * CHIPS + device // 2)
        for p in range(2):
            gain_ref[at + p : at + p + 1, :] = gain[device : device + 1, p * 128 : (p + 1) * 128]
    wide_goal[...] = in_goals(in_ref[...])
    near, far = out_goals(out_ref[...], core_ref[0])
    down_goal[0] = near
    down_goal[1] = far


def line_kernel(at_ref, *refs):
    for shift, ref in enumerate(refs[:4]):
        refs[-1][(at_ref[0] - shift) & 3] = ref[...]


def plane_kernel(at_ref, *refs):
    for shift, ref in enumerate(refs[:4]):
        for line in range(4):
            refs[-1][line * 4 + ((at_ref[0] - shift) & 3)] = ref[line]


def last_kernel(place_ref, taken_ref, own_ref, got_ref, *refs):
    made, out_ref = refs[:-1], refs[-1]
    groups = out_ref.shape[0] // ROWS
    for segment in range(len(made) - groups + 1):

        @pl.when(place_ref[0] == segment)
        def _():
            for group in range(groups):
                out_ref[group * ROWS : (group + 1) * ROWS, :] = made[group + segment][...]

    @pl.when(place_ref[0] == len(made) - groups + 1)
    def _():
        for group in range(groups - 1):
            at = len(made) - groups + 1 + group
            out_ref[group * ROWS : (group + 1) * ROWS, :] = made[at][...]
        produced = (taken_ref[...] + (own_ref[...] + got_ref[...])).astype(jnp.bfloat16)
        out_ref[(groups - 1) * ROWS :, :] = produced


VMEM = pl.BlockSpec(memory_space=pltpu.VMEM)
SMEM = pl.BlockSpec(memory_space=pltpu.SMEM)


def resident(weight):
    return pltpu.with_memory_space_constraint(weight, pltpu.VMEM)


def cost(products):
    return pl.CostEstimate(flops=2 * 128 * products, bytes_accessed=2 * MIB, transcendentals=0)


def prepare(core, x_in, norm_gain, in_index, out_index, x_order):
    groups = x_in.shape[0] // ROWS
    hbm = [pltpu.with_memory_space_constraint(v, pltpu.HBM) for v in (x_in, norm_gain, in_index, out_index)]
    return pl.pallas_call(
        functools.partial(prepare_kernel, groups),
        out_shape=[jax.ShapeDtypeStruct((2 * ROWS, 128), jnp.bfloat16)] * groups
        + [
            jax.ShapeDtypeStruct((4 * CHIPS, 128), jnp.float32),
            jax.ShapeDtypeStruct(in_index.shape, jnp.int32),
            jax.ShapeDtypeStruct((2,) + out_index.shape, jnp.int32),
        ],
        in_specs=[SMEM] + [pl.BlockSpec(memory_space=pltpu.HBM)] * 4 + [VMEM],
        out_specs=[VMEM] * (groups + 3),
        scratch_shapes=[pltpu.VMEM(v.shape, v.dtype) for v in (x_in, norm_gain, in_index, out_index)]
        + [pltpu.VMEM((2 * CHIPS, 256), jnp.float32), pltpu.SemaphoreType.DMA((4,))],
        compiler_params=pltpu.CompilerParams(vmem_limit_bytes=4 * MIB),
        name="prepare",
    )(core, *hbm, x_order)


def placed_by(kernel, at, parts, count):
    return pl.pallas_call(
        kernel,
        out_shape=jax.ShapeDtypeStruct((count,) + parts[0].shape[-2:], parts[0].dtype),
        in_specs=[SMEM] + [VMEM] * len(parts),
        out_specs=VMEM,
        compiler_params=pltpu.CompilerParams(vmem_limit_bytes=8 * MIB),
        name="placed",
    )(at, *parts)


def shifted_all(value, along_x):
    parts = [value]
    for shift in range(1, 4):
        pairs = []
        for x in range(4):
            for y in range(4):
                goal = ((x + shift) % 4 * 4 + y) if along_x else (x * 4 + (y + shift) % 4)
                pairs += [(2 * (x * 4 + y) + core, 2 * goal + core) for core in range(2)]
        parts.append(lax.ppermute(value, "tensor", pairs))
    return parts


def call_near(core, part, gain, weight):
    return pl.pallas_call(
        near_kernel,
        out_shape=(
            jax.ShapeDtypeStruct((2 * ROWS, GU_COLS), jnp.float32),
            jax.ShapeDtypeStruct((2 * ROWS, 128), jnp.float32),
        ),
        in_specs=[SMEM, VMEM, VMEM, VMEM],
        out_specs=(VMEM, VMEM),
        scratch_shapes=[pltpu.VMEM((2 * ROWS, GU_ROWS // 2), jnp.bfloat16)],
        compiler_params=pltpu.CompilerParams(vmem_limit_bytes=16 * MIB),
        cost_estimate=cost(GU_ROWS * GU_COLS // 2),
        name="near",
    )(core, part, gain, resident(weight))


def call_far(core, part, gain, weight, order, acc, square):
    return pl.pallas_call(
        far_kernel,
        out_shape=jax.ShapeDtypeStruct((CHIPS, KEPT, 256), jnp.bfloat16),
        in_specs=[SMEM] + [VMEM] * 6,
        out_specs=VMEM,
        scratch_shapes=[pltpu.VMEM((2 * ROWS, GU_ROWS // 2), jnp.bfloat16)],
        compiler_params=pltpu.CompilerParams(vmem_limit_bytes=16 * MIB),
        cost_estimate=cost(GU_ROWS * GU_COLS // 2),
        name="far",
    )(core, part, gain, resident(weight), order, acc, square)


def call_send(part, weight):
    return pl.pallas_call(
        send_kernel,
        out_shape=jax.ShapeDtypeStruct((ROWS, 256), jnp.float32),
        in_specs=[VMEM] * 2,
        out_specs=VMEM,
        compiler_params=pltpu.CompilerParams(vmem_limit_bytes=16 * MIB),
        cost_estimate=cost(DN_ROWS * DN_COLS // 2),
        name="send",
    )(part, resident(weight))


def call_own(part, weight, taken, back):
    return pl.pallas_call(
        own_kernel,
        out_shape=[jax.ShapeDtypeStruct((ROWS, 256), jnp.float32)] * 2,
        in_specs=[VMEM] * 4,
        out_specs=[VMEM] * 2,
        compiler_params=pltpu.CompilerParams(vmem_limit_bytes=16 * MIB),
        cost_estimate=cost(DN_ROWS * DN_COLS // 2),
        name="own",
    )(part, resident(weight), taken, back)


def call_finish(taken, own, got, order):
    return pl.pallas_call(
        finish_kernel,
        out_shape=(
            jax.ShapeDtypeStruct((ROWS, 256), jnp.bfloat16),
            jax.ShapeDtypeStruct((2 * ROWS, 128), jnp.bfloat16),
        ),
        in_specs=[VMEM] * 4,
        out_specs=(VMEM, VMEM),
        compiler_params=pltpu.CompilerParams(vmem_limit_bytes=4 * MIB),
        name="finish",
    )(taken, own, got, order)


def call_last(place, taken, own, got, made, groups):
    return pl.pallas_call(
        last_kernel,
        out_shape=jax.ShapeDtypeStruct((groups * ROWS, 256), jnp.bfloat16),
        in_specs=[SMEM] + [VMEM] * (3 + len(made)),
        out_specs=VMEM,
        compiler_params=pltpu.CompilerParams(vmem_limit_bytes=4 * MIB),
        name="last",
    )(place, taken, own, got, *made)


def orders():
    source = jnp.arange(256)
    goal = (source % 2) * 128 + source // 64 * 32 + source % 64 // 2
    x_order = (goal[:, None] == jnp.arange(256)[None, :]).astype(jnp.bfloat16)
    source = jnp.arange(512)
    goal = (source % 2) * 256 + source // 64 * 32 + source % 64 // 2
    h_order = (goal[:, None] == jnp.arange(512)[None, :]).astype(jnp.bfloat16)
    return x_order, h_order


def exchanged(value):
    same_core = [[2 * chip + core for chip in range(CHIPS)] for core in range(2)]
    return lax.all_to_all(value, "tensor", 0, 0, axis_index_groups=same_core)


def swapped(value):
    return lax.ppermute(value, "tensor", [(i, i ^ 1) for i in range(2 * CHIPS)])


def local(x_in, norm_gain, in_index, gate_blocks, up_blocks, out_index, down_blocks):
    segment_count = lax.axis_size("segment")
    segment_at = lax.axis_index("segment")
    tensor_at = lax.axis_index("tensor").astype(jnp.int32)
    core = (tensor_at & 1)[None]
    tokens = x_in.shape[0]
    group_count = tokens // ROWS
    tick_count = group_count + segment_count - 1
    x_order, h_order = orders()
    x_back = x_order.T
    in_index = jnp.transpose(in_index, (1, 0, 2))
    *firsts, gain, to_wide, to_down = prepare(core, x_in, norm_gain, in_index, out_index[0], x_order)
    is_first = jnp.broadcast_to(segment_at == 0, (8, 128)).astype(jnp.bfloat16)
    place = segment_at.astype(jnp.int32)[None]
    x_at, y_at = (tensor_at >> 3)[None], ((tensor_at >> 1) & 3)[None]
    core, place, x_at, y_at, x_order, x_back, h_order, firsts, gain, is_first = lax.optimization_barrier(
        (core, place, x_at, y_at, x_order, x_back, h_order, firsts, gain, is_first)
    )

    carried = None
    made = []
    hops = [(i, i + 1) for i in range(segment_count - 1)]
    for tick in range(tick_count):
        taken = firsts[min(tick, group_count - 1)]
        if carried is not None:
            taken = jnp.where(jnp.tile(is_first, (2 * ROWS // 8, 1)) > 0, taken, carried)
        if tick == 0:
            parts = shifted_all(taken, True)
            down, lent = densify_down(to_down, down_blocks[0])
            line = placed_by(line_kernel, x_at, parts + [resident(down)], 4)
            to_wide, line, lent = lax.optimization_barrier((to_wide, line, lent))
            borrowed = swapped(lent)
            parts = shifted_all(line, False)
            wide = densify_wide(to_wide, gate_blocks[0], up_blocks[0])
            mine = placed_by(plane_kernel, y_at, parts + [resident(wide)], CHIPS)
        else:
            mine = exchanged(jnp.broadcast_to(taken[None], (CHIPS, 2 * ROWS, 128)))
        other = swapped(mine)
        acc, square = call_near(core, mine, gain, wide)
        hidden = call_far(core, other, gain, wide, h_order, acc, square)
        mine = exchanged(hidden)
        got = swapped(call_send(mine, borrowed))
        residual, own = call_own(mine, down, taken, x_back)
        if tick + 1 == tick_count:
            return call_last(place, residual, own, got, made, group_count)[None]
        produced, ordered = call_finish(residual, own, got, x_order)
        made.append(produced)
        carried = lax.ppermute(ordered, "segment", hops)


def solution(mesh):
    placed = (
        P("replica", "tensor"),
        P("segment", None),
        P("segment", "tensor", None),
        P("segment", "tensor", None, None),
        P("segment", "tensor", None, None),
        P("segment", "tensor", None),
        P("segment", "tensor", None, None),
    )
    return jax.shard_map(
        local,
        mesh=mesh,
        in_specs=placed,
        out_specs=P("segment", "replica", "tensor"),
        check_vma=False,
    )
```
